32 devices in a mesh: chan: 4 (over y, core), blk: 8 (over z, x).
Axes of the slice: x: 2, y: 2, z: 4, core: 2. Of those that a mesh axis runs over, the one named last changes fastest.
Arguments:
- comp_alms: float32 [3, 4, 8, 4096], P(None, None, 'blk', 'chan'), may hold values from -6 to 6
- legendre: bfloat16 [2, 8, 4096, 32], P(None, 'blk'), may hold values from -0.09375 to 0.09375
- inv_noise: float32 [4, 2, 32, 8192], P('chan', None, 'blk'), may hold values from 0.5 to 5
- beam_window: float32 [4, 4096], replicated, may hold values from 0.1 to 1
- mixing: float32 [4, 3], replicated, may hold values from 0.2 to 1.5
- channel_of: int32 [4], replicated, may hold values from 0 to 3, each once
- m_orders: int32 [8], replicated, may hold values from 0 to 4095, as said below
- cycle_of: int32 [32], replicated, may hold values from 0 to 31, each once
- cycle_pixels: int32 [32], replicated, may hold values from 4 to 8192, as said below
Outputs:
- normal_product: float32 [3, 4, 8, 4096], P(None, None, 'blk', 'chan')
The draws below stay inside these ranges and needn't reach their ends.
Inputs may be any that keep to these rules, and one draw needn't show every extreme that they name: `m_orders`: the orders are distinct. `cycle_pixels`: each entry is 4 * min(h, 2048, 8192 - h) for some cycle number h of 1 to 8191; at least one entry equals 8192.
All inputs are finite; a program needn't handle non-finite values.
Results may differ from the reference program's by a relative error of at most 0.0022.
Values may be sent and summed in bfloat16 or wider, within the bound.
A program may use at most 128 MiB of HBM per device.

```python
import math
import jax
import jax.numpy as jnp
from jax import lax

L = 4096
PIX = 8192
NC = 3
CH = 4
M_TOT = 8
R_TOT = 32


def draw_m_orders(key, part):
    return jax.random.permutation(key, L)[:M_TOT].astype(jnp.int32)


def draw_cycle_pixels(key, part):
    first_key, second_key = jax.random.split(jax.random.fold_in(key, 17))
    numbers = jax.random.randint(first_key, (R_TOT,), 1, PIX).astype(jnp.int32)
    position = jax.random.randint(second_key, (), 0, R_TOT)
    numbers = numbers.at[position].set(PIX // 2)
    quarter = PIX // 4
    return (4 * jnp.minimum(jnp.minimum(numbers, quarter), PIX - numbers)).astype(jnp.int32)


def level_of(stream_key, extent, shards, least, high):
    gain = 1.0
    for dim, shards_of in shards:
        heights = jax.random.uniform(jax.random.fold_in(jax.random.fold_in(stream_key, 6), dim), (shards_of,), jnp.float32, least / len(shards), high / len(shards))
        gain = gain * jnp.repeat(jnp.exp(heights), extent[dim] // shards_of).reshape((-1,) + (1,) * (len(extent) - 1 - dim))
    return gain


def normal_values(rng, dims, deviation, bound, cuts=(), held_as=jnp.bfloat16):
    factor_of = level_of(rng, dims, cuts, -0.22, 0.18) if cuts else 1.0
    result = jax.random.normal(rng, dims, jnp.float32) * deviation * factor_of
    return jnp.minimum(jnp.maximum(result, -bound), bound).astype(held_as)


def setup_inputs(seed: int = 0) -> dict:
    key_list = jax.random.split(jax.random.key(seed), 10)
    comp_alms = normal_values(key_list[0], (NC, 4, M_TOT, L), 1.0, 6.0, ((2, 8), (3, 4)), jnp.float32)
    legendre = normal_values(key_list[1], (2, M_TOT, L, R_TOT), L ** -0.5, 0.09375, ((1, 8),))
    inv_noise = jnp.clip(jnp.exp(math.log(5.0) - 2.3025851 * jax.random.uniform(key_list[2], (CH, 2, R_TOT, PIX), jnp.float32) ** level_of(key_list[2], (CH, 2, R_TOT, PIX), ((0, 4), (2, 8)), -0.2, 0.2)), 0.5, 5.0)
    beam_window = jnp.clip(jax.random.uniform(key_list[3], (CH, L), jnp.float32, 0.1, 1.0), 0.1, 1.0)
    mixing = jnp.clip(jax.random.uniform(key_list[4], (CH, NC), jnp.float32, 0.2, 1.5), 0.2, 1.5)
    channel_of = jax.random.permutation(key_list[5], CH).astype(jnp.int32)
    m_orders = draw_m_orders(jax.random.fold_in(key_list[9], 71), 0)
    cycle_of = jax.random.permutation(key_list[7], R_TOT).astype(jnp.int32)
    cycle_pixels = draw_cycle_pixels(jax.random.fold_in(key_list[9], 71), 0)
    return {"comp_alms": comp_alms, "legendre": legendre, "inv_noise": inv_noise, "beam_window": beam_window, "mixing": mixing, "channel_of": channel_of, "m_orders": m_orders, "cycle_of": cycle_of, "cycle_pixels": cycle_pixels}


def phase_rows(orders, pix_count, cycle_width):
    columns = jnp.arange(cycle_width, dtype=jnp.int32)
    phase_steps = (orders[:, None] * (2 * columns[None, :] + 1)) % (2 * pix_count)
    angles = phase_steps.astype(jnp.float32) * (jnp.float32(math.pi) / pix_count.astype(jnp.float32))
    return jnp.concatenate([jnp.cos(angles), jnp.sin(angles)], axis=0).astype(jnp.bfloat16)


def combine_forward(plus_sum, minus_sum):
    return jnp.stack([plus_sum[:, 0] - minus_sum[:, 3], plus_sum[:, 1] + minus_sum[:, 2],
                      plus_sum[:, 2] + minus_sum[:, 1], plus_sum[:, 3] - minus_sum[:, 0]], axis=1)


def twist_grads(cycle_grads):
    return jnp.stack([-cycle_grads[:, 3], cycle_grads[:, 2], cycle_grads[:, 1], -cycle_grads[:, 0]], axis=1)


def cycle_work(coeffs, weights, orders, pix_count):
    slots = coeffs.shape[0]
    cycle_width = weights.shape[-1]
    phases = phase_rows(orders, pix_count, cycle_width)
    half_rows = phases.shape[0] // 2
    real_part = coeffs[:, 0::2]
    imag_part = coeffs[:, 1::2]
    stacked = jnp.concatenate([real_part, -imag_part], axis=2).reshape(2 * slots, 2 * half_rows)
    maps = jnp.dot(stacked, phases, preferred_element_type=jnp.float32)
    live_mask = jnp.arange(cycle_width, dtype=jnp.int32) < pix_count
    scaled = jnp.where(live_mask[None, None, :], weights, 0.0) / pix_count.astype(jnp.float32)
    weighted = (scaled.reshape(maps.shape) * maps).astype(jnp.bfloat16)
    returned = lax.dot_general(weighted, phases, (((1,), (1,)), ((), ())), preferred_element_type=jnp.float32)
    grad_real = returned[:, :half_rows].reshape(slots, 2, half_rows)
    grad_imag = (-returned[:, half_rows:]).reshape(slots, 2, half_rows)
    return jnp.stack([grad_real, grad_imag], axis=2).reshape(slots, 4, half_rows).astype(jnp.bfloat16)


def mix_components(mix_rows, components):
    accum = mix_rows[:, 0, None, None, None] * components[0][None]
    for comp_index in range(1, components.shape[0]):
        accum = accum + mix_rows[:, comp_index, None, None, None] * components[comp_index][None]
    return accum


def reference(comp_alms, legendre, inv_noise, beam_window, mixing, channel_of, m_orders, cycle_of, cycle_pixels):
    length = legendre.shape[2]
    cycle_total = legendre.shape[3]
    mix_rows = jnp.take(mixing, channel_of, axis=0)
    beam_rows = jnp.take(beam_window, channel_of, axis=0)
    keep_mask = (jnp.arange(length, dtype=jnp.int32)[None, :] >= m_orders[:, None]).astype(jnp.float32)
    mixed_alm = mix_components(mix_rows, comp_alms)
    chan_alm = (mixed_alm * beam_rows[:, None, None, :] * keep_mask[None, None]).astype(jnp.bfloat16)
    channels = chan_alm.shape[0]

    def forward_order(index):
        tables = lax.dynamic_index_in_dim(legendre, index, 1, keepdims=False)
        row_block = lax.dynamic_index_in_dim(chan_alm, index, 2, keepdims=False).reshape(channels * 4, length)
        plus_sum = jnp.dot(row_block, tables[0], preferred_element_type=jnp.float32).reshape(channels, 4, cycle_total)
        minus_sum = jnp.dot(row_block, tables[1], preferred_element_type=jnp.float32).reshape(channels, 4, cycle_total)
        return combine_forward(plus_sum, minus_sum)

    cycle_coeffs = lax.map(forward_order, jnp.arange(M_TOT, dtype=jnp.int32))
    cycle_coeffs = jnp.transpose(cycle_coeffs, (1, 2, 0, 3)).astype(jnp.bfloat16)
    slot_coeffs = jnp.take(cycle_coeffs, cycle_of, axis=3)

    def per_cycle(slot):
        coeffs = lax.dynamic_index_in_dim(slot_coeffs, slot, 3, keepdims=False)
        weights = lax.dynamic_index_in_dim(inv_noise, slot, 2, keepdims=False)
        pix_count = cycle_pixels[cycle_of[slot]]
        return cycle_work(coeffs, weights, m_orders, pix_count)

    slot_grads = lax.map(per_cycle, jnp.arange(R_TOT, dtype=jnp.int32))
    slot_grads = jnp.transpose(slot_grads, (1, 2, 3, 0))
    cycle_grads = jnp.zeros_like(slot_grads).at[:, :, :, cycle_of].set(slot_grads)

    def adjoint_order(index):
        tables = lax.dynamic_index_in_dim(legendre, index, 1, keepdims=False)
        order_grads = lax.dynamic_index_in_dim(cycle_grads, index, 2, keepdims=False)
        twisted = twist_grads(order_grads)
        accum = lax.dot_general(order_grads.reshape(channels * 4, cycle_total), tables[0], (((1,), (1,)), ((), ())), preferred_element_type=jnp.float32)
        accum = accum + lax.dot_general(twisted.reshape(channels * 4, cycle_total), tables[1], (((1,), (1,)), ((), ())), preferred_element_type=jnp.float32)
        return accum.reshape(channels, 4, length)

    alm_grads = lax.map(adjoint_order, jnp.arange(M_TOT, dtype=jnp.int32))
    alm_grads = jnp.transpose(alm_grads, (1, 2, 0, 3)) * keep_mask[None, None]
    beamed = alm_grads * beam_rows[:, None, None, :]
    return jnp.einsum('kc,kpml->cpml', mix_rows, beamed, precision=lax.Precision.HIGHEST)
```

```python
import functools
import math

import jax
import jax.numpy as jnp
from jax import lax
from jax.experimental import pallas as pl
from jax.experimental.pallas import tpu as pltpu
from jax.sharding import PartitionSpec as P

F32 = jnp.float32
BF16 = jnp.bfloat16
LANES = 128
NT = (((1,), (1,)), ((), ()))
NN = (((1,), (0,)), ((), ()))


def iota(shape, dim):
    return lax.broadcasted_iota(jnp.int32, shape, dim)


def dot(left, right, dims):
    return lax.dot_general(left, right, dims, preferred_element_type=F32)


def exact_mod(value, modulus, inverse):
    rest = value - jnp.floor(value * inverse) * modulus
    rest = jnp.where(rest < 0, rest + modulus, rest)
    return jnp.where(rest >= modulus, rest - modulus, rest)


def kernel(
    chans, blks, alm_hbm, leg_hbm, inv_hbm, beam_hbm, mix_hbm, chan_hbm, order_hbm, cycle_hbm,
    pixel_hbm, cycle_row_hbm, out_ref, mix_s, chan_s, order_s, cycle_s, pixel_s, cycle_row, comp_v,
    leg_v, inv_v, beam_v, gain_v, phases, fold_v, send1, recv1, send2, recv2, spare1, spare2, twin_v,
    in_sem, send_sem, recv_sem,
):
    comps = comp_v.shape[0]
    shard = comp_v.shape[2]
    cycles = leg_v.shape[1]
    slots = inv_v.shape[0] // 2
    width = inv_v.shape[1]
    rows = 4 * chans
    lanes = 4 * cycles
    total = chans * blks
    me_c = lax.axis_index("chan")
    me_b = lax.axis_index("blk")
    first = pl.multiple_of(me_c * shard, shard)

    def peer(offset):
        return lax.rem(me_c + offset // blks, chans), lax.rem(me_b + offset % blks, blks)

    def each_peer(act):
        if total <= 64:
            for offset in range(1, total):
                act(offset)
        else:
            lax.fori_loop(1, total, lambda offset, carry: (act(offset), carry)[1], 0)

    barrier = pltpu.get_barrier_semaphore()

    def greet(offset):
        pl.semaphore_signal(
            barrier, inc=1, device_id=peer(offset), device_id_type=pl.DeviceIdType.MESH
        )

    scalars = []

    def load(src, dst, group):
        copy = pltpu.make_async_copy(src, dst, in_sem.at[group])
        copy.start()
        return copy

    def loaded(dst, group):
        pltpu.make_async_copy(dst, dst, in_sem.at[group]).wait()

    for src, dst in (
        (order_hbm, order_s), (cycle_hbm, cycle_s), (pixel_hbm, pixel_s), (mix_hbm, mix_s),
        (chan_hbm, chan_s), (cycle_row_hbm, cycle_row),
    ):
        scalars.append(load(src, dst, 4 + len(scalars)))
    for kind in range(2):
        load(leg_hbm.at[kind, 0, :, pl.ds(first, shard)], leg_v.at[kind], 2)
    for comp in range(comps):
        for part in range(4):
            for half in range(2):
                load(alm_hbm.at[comp, part], comp_v.at[comp, pl.ds(4 * half + part, 1), :], 0)
    load(beam_hbm.at[:, pl.ds(first, shard)], beam_v, 1)
    for stokes in range(2):
        load(inv_hbm.at[0, stokes], inv_v.at[pl.ds(stokes * slots, slots), :], 3)
    each_peer(greet)
    for copy in scalars:
        copy.wait()

    own_cycles = [cycle_s[me_b * slots + slot] for slot in range(slots)]
    own_pixels = [pixel_s[cycle].astype(F32) for cycle in own_cycles]

    def by_slot(slot_index, values):
        result = jnp.where(slot_index == 0, values[0], values[slots - 1])
        for slot in range(1, slots - 1):
            result = jnp.where(slot_index == slot, values[slot], result)
        return result

    grid = (slots * blks, LANES)
    row = iota(grid, 0)
    lane = iota(grid, 1).astype(F32)
    pixels = by_slot(row // blks, own_pixels)
    orders = jnp.zeros(grid, F32)
    for order in range(blks):
        orders = jnp.where(row % blks == order, order_s[order].astype(F32), orders)
    modulus = 2.0 * pixels
    inverse = 1.0 / modulus
    scale = jnp.float32(math.pi) / pixels
    fine = exact_mod(orders * (2.0 * lane + 1.0), modulus, inverse) * scale
    stride = exact_mod(orders * (2.0 * LANES), modulus, inverse)
    coarse = exact_mod(stride * lane, modulus, inverse) * scale
    fine_cos, fine_sin = jnp.cos(fine), jnp.sin(fine)
    coarse_cos, coarse_sin = jnp.cos(coarse), jnp.sin(coarse)
    for chunk in range(width // LANES):
        window = pl.ds(chunk * LANES, LANES)
        turn_cos = coarse_cos[:, chunk : chunk + 1]
        turn_sin = coarse_sin[:, chunk : chunk + 1]
        real = turn_cos * fine_cos - turn_sin * fine_sin
        imag = turn_sin * fine_cos + turn_cos * fine_sin
        for slot in range(slots):
            own = slice(slot * blks, (slot + 1) * blks)
            both = jnp.concatenate([real[own], imag[own]], axis=0)
            phases[pl.ds(slot * 2 * blks, 2 * blks), window] = both.astype(BF16)

    loaded(comp_v, 0)
    loaded(beam_v, 1)
    loaded(leg_v, 2)
    low_half = iota((8, 1), 0) < 4
    keep = (iota((1, shard), 1) + first >= order_s[me_b]).astype(F32)
    alm_rows = []
    for pair in range(chans // 2):
        picked = [chan_s[2 * pair], chan_s[2 * pair + 1]]
        columns = [
            jnp.where(low_half, mix_s[picked[0], comp], mix_s[picked[1], comp])
            for comp in range(comps)
        ]
        mixed = columns[0] * comp_v[0]
        for comp in range(1, comps):
            mixed = mixed + columns[comp] * comp_v[comp]
        gains = [beam_v[pl.ds(chan, 1), :] * keep for chan in picked]
        gain_v[pl.ds(2 * pair, 1), :] = gains[0]
        gain_v[pl.ds(2 * pair + 1, 1), :] = gains[1]
        alm_rows.append(mixed * jnp.where(low_half, gains[0], gains[1]))
    alm = jnp.concatenate(alm_rows, axis=0).astype(BF16)
    plus = dot(alm, jnp.concatenate([leg_v[0]] * 4, axis=0), NT)
    minus = dot(alm, jnp.concatenate([leg_v[1]] * 4, axis=0), NT)
    row_part = iota(plus.shape, 0) % 4
    lane_part = iota(plus.shape, 1) // cycles
    outer = (lane_part == 0) | (lane_part == 3)
    signed = jnp.where(outer, -minus, minus)
    joined = jnp.where(lane_part == row_part, plus, 0.0) + jnp.where(
        lane_part == 3 - row_part, signed, 0.0
    )
    folded = joined
    for step in range(1, 4):
        folded = folded + pltpu.roll(joined, rows - step, 0)
    for chan in range(chans):
        send1[pl.ds(chan, 1), :] = folded[4 * chan : 4 * chan + 1]

    pl.semaphore_wait(barrier, total - 1)

    def scatter(src_of, dst_of, own_spare, phase):
        def start(offset):
            dest_c, dest_b = peer(offset)
            pltpu.make_async_remote_copy(
                src_ref=src_of(dest_b),
                dst_ref=dst_of(),
                send_sem=send_sem.at[phase],
                recv_sem=recv_sem.at[phase],
                device_id=(dest_c, dest_b),
                device_id_type=pl.DeviceIdType.MESH,
            ).start()

        each_peer(start)
        pltpu.make_async_copy(src_of(me_b), dst_of(), recv_sem.at[phase]).start()
        pltpu.make_async_copy(src_of(me_b), own_spare, send_sem.at[phase]).start()

    def arrived(dst, phase):
        pltpu.make_async_copy(dst, dst, recv_sem.at[phase]).wait()

    def sent(dst, phase):
        pltpu.make_async_copy(dst, dst, send_sem.at[phase]).wait()

    scatter(lambda dest_b: send1, lambda: recv1.at[me_c, me_b], spare1, 0)

    loaded(inv_v, 3)
    grid = (2 * slots, width)
    live = iota(grid, 1).astype(F32) < by_slot(iota((2 * slots, 1), 0) % slots, own_pixels)
    inv_v[...] = jnp.where(live, inv_v[...], 0.0)
    piece = min(1024, width)
    gram = None
    for index in range(width // piece):
        window = pl.ds(index * piece, piece)
        table = phases[:, window]
        blocks = []
        for slot in range(slots):
            for stokes in range(2):
                noise = inv_v[pl.ds(stokes * slots + slot, 1), window]
                wide = jnp.broadcast_to(noise, (2 * blks, piece)).astype(BF16)
                blocks.append(wide * table[slot * 2 * blks : (slot + 1) * 2 * blks])
        term = dot(table, jnp.concatenate(blocks, axis=0), NT)
        gram = term if gram is None else gram + term
    out_row = iota((2 * blks, lanes), 0)
    out_lane = iota((2 * blks, lanes), 1)
    lane_slot = out_lane // (4 * blks)
    picked_gram = gram[0 : 2 * blks]
    for slot in range(1, slots):
        picked_gram = jnp.where(
            lane_slot == slot, gram[slot * 2 * blks : (slot + 1) * 2 * blks], picked_gram
        )
    odd = (out_row // blks) != ((out_lane // blks) % 2)
    weight = 1.0 / by_slot(lane_slot, own_pixels)
    picked_gram = picked_gram * jnp.where(odd, -weight, weight)
    send2[0] = picked_gram[0:blks]
    send2[1] = picked_gram[blks : 2 * blks]
    scatter(
        lambda dest_b: send2.at[:, dest_b, :],
        lambda: recv2.at[me_b, pl.ds(2 * me_c, 2), :],
        spare2,
        1,
    )

    to_lane = iota((cycles, lanes), 1)
    spread = (
        iota((cycles, lanes), 0) == (to_lane % blks) * slots + to_lane // (4 * blks)
    ).astype(F32).astype(BF16)
    lane_cycle = dot(
        jnp.broadcast_to(cycle_row[...].astype(F32), (8, cycles)).astype(BF16), spread, NN
    )[0:1]
    from_row = iota((lanes, lanes), 0)
    square_lane = iota((lanes, lanes), 1)
    shuffle = (
        ((from_row % cycles).astype(F32) == lane_cycle)
        & (from_row // cycles == (square_lane // blks) % 4)
    ).astype(F32)
    leg_stack = jnp.concatenate([leg_v[0], leg_v[1]] * 2, axis=0)
    back_leg = dot(shuffle.T.astype(BF16), leg_stack, NN).astype(BF16)
    shuffle = shuffle.astype(BF16)

    arrived(recv1, 0)
    gathered = []
    for order in range(blks):
        coeffs = recv1[0, order]
        for chan in range(1, chans):
            coeffs = coeffs + recv1[chan, order]
        gathered.append(coeffs)
    coeffs = dot(jnp.concatenate(gathered, axis=0).astype(BF16), shuffle, NN)
    for order in range(blks):
        own = coeffs[order * chans : (order + 1) * chans]
        for tile in range(lanes // LANES):
            for part in range(2):
                twin_v[order, tile, pl.ds(part, chans, stride=2), :] = own[
                    :, tile * LANES : (tile + 1) * LANES
                ]
    turned = [
        jnp.concatenate([twin_v[order, tile] for tile in range(lanes // LANES)], axis=1)
        for order in range(blks)
    ]
    low_lane = iota((2 * chans, lanes), 1) % blks
    step = 1
    while step < blks:
        upper = (low_lane // step) % 2 == 1
        following = list(turned)
        for order in range(blks):
            if (order // step) % 2 == 0:
                one, two = turned[order], turned[order + step]
                following[order] = jnp.where(upper, pltpu.roll(two, step, 1), one)
                following[order + step] = jnp.where(
                    upper, two, pltpu.roll(one, lanes - step, 1)
                )
        turned = following
        step *= 2

    final_row = iota((8, lanes), 0)
    final_lane = iota((8, lanes), 1)
    row_real = final_row % 2
    row_stokes = (final_row // 2) % 2
    lane_kind = (final_lane // blks) % 2
    lane_stokes = (final_lane // (2 * blks)) % 2
    straight = (lane_kind == 0) & (lane_stokes == row_stokes)
    crossed = (lane_kind == 1) & (lane_stokes != row_stokes)
    cross_sign = jnp.where(row_stokes == row_real, -1.0, 1.0)
    mask = [
        jnp.where(straight & (row_real == real), 1.0, 0.0)
        + jnp.where(crossed & (row_real != real), cross_sign, 0.0)
        for real in range(2)
    ]

    arrived(recv2, 1)
    sums = [recv2[block] * turned[block] for block in range(blks)]
    step = blks // 2
    while step >= 1:
        upper = (low_lane // step) % 2 == 1
        merged = []
        for block in range(step):
            one, two = sums[block], sums[block + step]
            kept = jnp.where(upper, two, one)
            moved = jnp.where(upper, one, two)
            merged.append(
                kept
                + jnp.where(
                    upper, pltpu.roll(moved, step, 1), pltpu.roll(moved, lanes - step, 1)
                )
            )
        sums = merged
        step //= 2
    total_sum = sums[0]
    odd_part = (iota(total_sum.shape, 1) // blks) % 2 == 1
    total_sum = total_sum + jnp.where(
        odd_part, pltpu.roll(total_sum, blks, 1), pltpu.roll(total_sum, lanes - blks, 1)
    )
    total_sum = total_sum.astype(BF16).astype(F32)
    left = jnp.concatenate(
        [
            mask[0] * total_sum[2 * chan : 2 * chan + 1]
            + mask[1] * total_sum[2 * chan + 1 : 2 * chan + 2]
            for chan in range(chans)
        ],
        axis=0,
    )
    alm_grads = dot(left.astype(BF16), back_leg, NN)
    scaled = [
        alm_grads[8 * chan : 8 * chan + 8] * gain_v[pl.ds(chan, 1), :] for chan in range(chans)
    ]
    for comp in range(comps):
        mixed = mix_s[chan_s[0], comp] * scaled[0]
        for chan in range(1, chans):
            mixed = mixed + mix_s[chan_s[chan], comp] * scaled[chan]
        out_ref[comp] = mixed[0:4]
    sent(recv1, 0)
    sent(recv2, 1)


def body(
    chans, blks, comp_alms, legendre, inv_noise, beam_window, mixing, channel_of, m_orders,
    cycle_of, cycle_pixels,
):
    comps, parts, order_dev, shard = comp_alms.shape
    cycles = legendre.shape[3]
    chan_dev, stokes, slots, width = inv_noise.shape
    assert parts == 4 and stokes == 2 and order_dev == 1 and chan_dev == 1
    lanes = 4 * cycles
    assert slots * blks == cycles
    any_space = pl.BlockSpec(memory_space=pl.ANY)
    vector = pl.BlockSpec(memory_space=pltpu.VMEM)
    result = pl.pallas_call(
        functools.partial(kernel, chans, blks),
        out_shape=pltpu.VMEM((comps, 4, shard), F32),
        in_specs=[any_space] * 10,
        out_specs=vector,
        scratch_shapes=[
            pltpu.SMEM(mixing.shape, F32),
            pltpu.SMEM(channel_of.shape, jnp.int32),
            pltpu.SMEM(m_orders.shape, jnp.int32),
            pltpu.SMEM(cycle_of.shape, jnp.int32),
            pltpu.SMEM(cycle_pixels.shape, jnp.int32),
            pltpu.VMEM((1, cycles), jnp.int32),
            pltpu.VMEM((comps, 8, shard), F32),
            pltpu.VMEM((2, cycles, shard), BF16),
            pltpu.VMEM((2 * slots, width), F32),
            pltpu.VMEM((beam_window.shape[0], shard), F32),
            pltpu.VMEM((chans, shard), F32),
            pltpu.VMEM((2 * slots * blks, width), BF16),
            pltpu.VMEM((4 * chans, lanes), F32),
            pltpu.VMEM((chans, lanes), F32),
            pltpu.VMEM((chans, blks, chans, lanes), F32),
            pltpu.VMEM((2, blks, lanes), F32),
            pltpu.VMEM((blks, 2 * chans, lanes), F32),
            pltpu.VMEM((chans, lanes), F32),
            pltpu.VMEM((2, lanes), F32),
            pltpu.VMEM((blks, lanes // LANES, 2 * chans, LANES), F32),
            pltpu.SemaphoreType.DMA((10,)),
            pltpu.SemaphoreType.DMA((2,)),
            pltpu.SemaphoreType.DMA((2,)),
        ],
        compiler_params=pltpu.CompilerParams(collective_id=0, has_side_effects=True),
        name="normal_product",
    )(
        comp_alms, jnp.swapaxes(legendre, 2, 3), inv_noise, beam_window, mixing, channel_of,
        m_orders, cycle_of, cycle_pixels, cycle_of.reshape(1, cycles),
    )
    return result.reshape(comp_alms.shape)


def solution(mesh):
    in_specs = (
        P(None, None, "blk", "chan"),
        P(None, "blk", None, None),
        P("chan", None, "blk", None),
        P(),
        P(),
        P(),
        P(),
        P(),
        P(),
    )
    out_specs = P(None, None, "blk", "chan")
    work = functools.partial(body, mesh.shape["chan"], mesh.shape["blk"])
    return jax.shard_map(work, mesh=mesh, in_specs=in_specs, out_specs=out_specs, check_vma=False)
```

```python
import functools
import math

import jax
import jax.numpy as jnp
from jax import lax
from jax.experimental import pallas as pl
from jax.experimental.pallas import tpu as pltpu
from jax.sharding import PartitionSpec as P

F32 = jnp.float32
BF16 = jnp.bfloat16
LANES = 128
NT = (((1,), (1,)), ((), ()))
NN = (((1,), (0,)), ((), ()))


def iota(shape, dim):
    return lax.broadcasted_iota(jnp.int32, shape, dim)


def dot(left, right, dims):
    return lax.dot_general(left, right, dims, preferred_element_type=F32)


def exact_mod(value, modulus, inverse):
    rest = value - jnp.floor(value * inverse) * modulus
    rest = jnp.where(rest < 0, rest + modulus, rest)
    return jnp.where(rest >= modulus, rest - modulus, rest)


def turn(steps, count, double_inverse):
    quarter = jnp.floor(steps * double_inverse + 0.5)
    angle = (2.0 * steps - quarter * count) * (double_inverse * jnp.float32(math.pi / 4))
    square = angle * angle
    sine = angle + angle * square * (
        (-1.9515295891e-4 * square + 8.3321608736e-3) * square - 1.6666654611e-1
    )
    cosine = (1.0 - 0.5 * square) + square * square * (
        (2.443315711809948e-5 * square - 1.388731625493765e-3) * square + 4.166664568298827e-2
    )
    index = quarter.astype(jnp.int32)
    odd = index % 2 == 1
    real = jnp.where(odd, sine, cosine)
    imag = jnp.where(odd, cosine, sine)
    real = jnp.where((index + 1) // 2 % 2 == 1, -real, real)
    imag = jnp.where(index // 2 % 2 == 1, -imag, imag)
    return real, imag


def pair_turns(cosines, sines, order):
    cos_one, sin_one = cosines[order : order + 1], sines[order : order + 1]
    cos_cos, sin_sin = cos_one * cosines, sin_one * sines
    sin_cos, cos_sin = sin_one * cosines, cos_one * sines
    return [cos_cos - sin_sin, sin_cos + cos_sin, cos_cos + sin_sin, sin_cos - cos_sin]


def kernel(
    chans, blks, alm_hbm, leg_hbm, inv_hbm, beam_hbm, mix_hbm, chan_hbm, order_hbm, cycle_hbm,
    pixel_hbm, cycle_row_hbm, out_ref, mix_s, chan_s, order_s, cycle_s, pixel_s, cycle_row, comp_v,
    leg_v, inv_v, beam_v, gain_v, fine_v, coarse_v, send1, recv1, send2, recv2, spare1, spare2, twin_v,
    in_sem, send_sem, recv_sem,
):
    comps = comp_v.shape[0]
    shard = comp_v.shape[2]
    cycles = leg_v.shape[1]
    slots = inv_v.shape[0]
    chunks = inv_v.shape[1] // 2
    rows = 4 * chans
    lanes = 4 * cycles
    total = chans * blks
    me_c = lax.axis_index("chan")
    me_b = lax.axis_index("blk")
    first = pl.multiple_of(me_c * shard, shard)

    def peer(offset):
        return lax.rem(me_c + offset // blks, chans), lax.rem(me_b + offset % blks, blks)

    def each_peer(act):
        if total <= 64:
            for offset in range(1, total):
                act(offset)
        else:
            lax.fori_loop(1, total, lambda offset, carry: (act(offset), carry)[1], 0)

    barrier = pltpu.get_barrier_semaphore()

    def greet(offset):
        pl.semaphore_signal(
            barrier, inc=1, device_id=peer(offset), device_id_type=pl.DeviceIdType.MESH
        )

    scalars = []

    def load(src, dst, group):
        copy = pltpu.make_async_copy(src, dst, in_sem.at[group])
        copy.start()
        return copy

    def loaded(dst, group):
        pltpu.make_async_copy(dst, dst, in_sem.at[group]).wait()

    for src, dst in (
        (order_hbm, order_s), (cycle_hbm, cycle_s), (pixel_hbm, pixel_s), (mix_hbm, mix_s),
        (chan_hbm, chan_s), (cycle_row_hbm, cycle_row),
    ):
        scalars.append(load(src, dst, 4 + len(scalars)))
    for kind in range(2):
        load(leg_hbm.at[kind, 0, :, pl.ds(first, shard)], leg_v.at[kind], 2)
    for comp in range(comps):
        for part in range(4):
            for half in range(2):
                load(alm_hbm.at[comp, part], comp_v.at[comp, pl.ds(4 * half + part, 1), :], 0)
    load(beam_hbm.at[:, pl.ds(first, shard)], beam_v, 1)
    for stokes in range(2):
        for slot in range(slots):
            load(
                inv_hbm.at[stokes, :, slot, :],
                inv_v.at[slot, pl.ds(stokes * chunks, chunks), :],
                3,
            )
    each_peer(greet)
    for copy in scalars:
        copy.wait()

    own_cycles = [cycle_s[me_b * slots + slot] for slot in range(slots)]
    own_pixels = [pixel_s[cycle].astype(F32) for cycle in own_cycles]

    def by_slot(slot_index, values):
        result = jnp.where(slot_index == 0, values[0], values[slots - 1])
        for slot in range(1, slots - 1):
            result = jnp.where(slot_index == slot, values[slot], result)
        return result

    grid = (slots * blks, LANES)
    row = iota(grid, 0)
    lane = iota(grid, 1).astype(F32)
    pixels = by_slot(row // blks, own_pixels)
    orders = jnp.zeros(grid, F32)
    for order in range(blks):
        orders = jnp.where(row % blks == order, order_s[order].astype(F32), orders)
    modulus = 2.0 * pixels
    reciprocal = 1.0 / pixels
    inverse = 0.5 * reciprocal
    double_inverse = 2.0 * reciprocal
    chunk = (iota(grid, 1) % chunks).astype(F32)
    fine = exact_mod(orders * (2.0 * lane + 1.0), modulus, inverse)
    stride = exact_mod(orders * (2.0 * LANES), modulus, inverse)
    coarse = exact_mod(stride * chunk, modulus, inverse)
    fine_cos, fine_sin = turn(fine, pixels, double_inverse)
    coarse_cos, coarse_sin = turn(coarse, pixels, double_inverse)
    for slot in range(slots):
        own = slice(slot * blks, (slot + 1) * blks)
        for order in range(blks):
            block = pl.ds(order * 4 * blks, 4 * blks)
            fine_v[slot, block, :] = jnp.concatenate(
                pair_turns(fine_cos[own], fine_sin[own], order), axis=0
            ).astype(BF16)
            coarse_v[slot, block, :] = jnp.concatenate(
                pair_turns(coarse_cos[own], coarse_sin[own], order), axis=0
            )

    loaded(comp_v, 0)
    loaded(beam_v, 1)
    loaded(leg_v, 2)
    low_half = iota((8, 1), 0) < 4
    keep = (iota((1, shard), 1) + first >= order_s[me_b]).astype(F32)
    alm_rows = []
    for pair in range(chans // 2):
        picked = [chan_s[2 * pair], chan_s[2 * pair + 1]]
        columns = [
            jnp.where(low_half, mix_s[picked[0], comp], mix_s[picked[1], comp])
            for comp in range(comps)
        ]
        mixed = columns[0] * comp_v[0]
        for comp in range(1, comps):
            mixed = mixed + columns[comp] * comp_v[comp]
        gains = [beam_v[pl.ds(chan, 1), :] * keep for chan in picked]
        gain_v[pl.ds(2 * pair, 1), :] = gains[0]
        gain_v[pl.ds(2 * pair + 1, 1), :] = gains[1]
        alm_rows.append(mixed * jnp.where(low_half, gains[0], gains[1]))
    alm = jnp.concatenate(alm_rows, axis=0).astype(BF16)
    plus = dot(alm, jnp.concatenate([leg_v[0]] * 4, axis=0), NT)
    minus = dot(alm, jnp.concatenate([leg_v[1]] * 4, axis=0), NT)
    row_part = iota(plus.shape, 0) % 4
    lane_part = iota(plus.shape, 1) // cycles
    outer = (lane_part == 0) | (lane_part == 3)
    signed = jnp.where(outer, -minus, minus)
    joined = jnp.where(lane_part == row_part, plus, 0.0) + jnp.where(
        lane_part == 3 - row_part, signed, 0.0
    )
    folded = joined
    for step in range(1, 4):
        folded = folded + pltpu.roll(joined, rows - step, 0)
    for chan in range(chans):
        send1[pl.ds(chan, 1), :] = folded[4 * chan : 4 * chan + 1]

    pl.semaphore_wait(barrier, total - 1)

    def scatter(src_of, dst_of, own_spare, phase):
        def start(offset):
            dest_c, dest_b = peer(offset)
            pltpu.make_async_remote_copy(
                src_ref=src_of(dest_b),
                dst_ref=dst_of(),
                send_sem=send_sem.at[phase],
                recv_sem=recv_sem.at[phase],
                device_id=(dest_c, dest_b),
                device_id_type=pl.DeviceIdType.MESH,
            ).start()

        each_peer(start)
        pltpu.make_async_copy(src_of(me_b), dst_of(), recv_sem.at[phase]).start()
        pltpu.make_async_copy(src_of(me_b), own_spare, send_sem.at[phase]).start()

    def arrived(dst, phase):
        pltpu.make_async_copy(dst, dst, recv_sem.at[phase]).wait()

    def sent(dst, phase):
        pltpu.make_async_copy(dst, dst, send_sem.at[phase]).wait()

    scatter(lambda dest_b: send1, lambda: recv1.at[me_c, me_b], spare1, 0)

    loaded(inv_v, 3)
    grid = (2 * chunks, LANES)
    pixel_index = (iota(grid, 0) % chunks) * LANES + iota(grid, 1)
    parts = [[] for _ in range(blks)]
    for slot in range(slots):
        live = pixel_index.astype(F32) < own_pixels[slot]
        noise = jnp.where(live, inv_v[slot], 0.0).astype(BF16)
        inner = dot(fine_v[slot], noise, NT)
        for order in range(blks):
            base = order * 4 * blks
            held = [inner[base + kind * blks : base + (kind + 1) * blks] for kind in range(4)]
            outer_turn = [
                coarse_v[slot, pl.ds(base + kind * blks, blks), :] for kind in range(4)
            ]
            add_real = outer_turn[0] * held[0] - outer_turn[1] * held[1]
            add_imag = outer_turn[0] * held[1] + outer_turn[1] * held[0]
            sub_real = outer_turn[2] * held[2] - outer_turn[3] * held[3]
            sub_imag = outer_turn[2] * held[3] + outer_turn[3] * held[2]
            parts[order].append(
                jnp.concatenate(
                    [
                        sub_real + add_real,
                        sub_imag - add_imag,
                        -sub_imag - add_imag,
                        sub_real - add_real,
                    ],
                    axis=0,
                ).astype(BF16)
            )
    ones = (iota((8, LANES), 1) // chunks == iota((8, LANES), 0)).astype(F32).astype(BF16)
    weight = 0.5 / by_slot(iota((2, lanes), 1) // (4 * blks), own_pixels)
    for order in range(blks):
        summed = dot(ones, jnp.concatenate(parts[order], axis=0), NT)
        send2[order] = summed[0:2] * weight
    scatter(
        lambda dest_b: send2.at[dest_b],
        lambda: recv2.at[me_b, pl.ds(2 * me_c, 2), :],
        spare2,
        1,
    )

    to_lane = iota((cycles, lanes), 1)
    spread = (
        iota((cycles, lanes), 0) == (to_lane % blks) * slots + to_lane // (4 * blks)
    ).astype(F32).astype(BF16)
    lane_cycle = dot(
        jnp.broadcast_to(cycle_row[...].astype(F32), (8, cycles)).astype(BF16), spread, NN
    )[0:1]
    half = (2 * cycles, lanes)
    from_row = iota(half, 0)
    shuffle = (
        ((from_row % cycles).astype(F32) == lane_cycle)
        & (from_row // cycles == (iota(half, 1) // blks) % 2)
    ).astype(F32)
    leg_stack = jnp.concatenate([leg_v[0], leg_v[1]], axis=0)
    back_leg = dot(shuffle.T.astype(BF16), leg_stack, NN).astype(BF16)
    empty = jnp.zeros(half, F32)
    shuffle = jnp.concatenate(
        [
            jnp.concatenate([shuffle, empty], axis=1),
            jnp.concatenate([empty, shuffle], axis=1),
        ],
        axis=0,
    ).astype(BF16)

    arrived(recv1, 0)
    gathered = []
    for order in range(blks):
        coeffs = recv1[0, order]
        for chan in range(1, chans):
            coeffs = coeffs + recv1[chan, order]
        gathered.append(coeffs)
    coeffs = dot(jnp.concatenate(gathered, axis=0).astype(BF16), shuffle, NN)
    for order in range(blks):
        own = coeffs[order * chans : (order + 1) * chans]
        for tile in range(lanes // LANES):
            for part in range(2):
                begin = part * lanes + tile * LANES
                twin_v[order, tile, pl.ds(part, chans, stride=2), :] = own[
                    :, begin : begin + LANES
                ]
    turned = [
        jnp.concatenate([twin_v[order, tile] for tile in range(lanes // LANES)], axis=1)
        for order in range(blks)
    ]
    low_lane = iota((2 * chans, lanes), 1) % blks
    step = 1
    while step < blks:
        upper = (low_lane // step) % 2 == 1
        following = list(turned)
        for order in range(blks):
            if (order // step) % 2 == 0:
                one, two = turned[order], turned[order + step]
                following[order] = jnp.where(upper, pltpu.roll(two, step, 1), one)
                following[order + step] = jnp.where(
                    upper, two, pltpu.roll(one, lanes - step, 1)
                )
        turned = following
        step *= 2

    final_row = iota((8, lanes), 0)
    final_lane = iota((8, lanes), 1)
    row_real = final_row % 2
    row_stokes = (final_row // 2) % 2
    lane_kind = (final_lane // blks) % 2
    lane_real = (final_lane // (2 * blks)) % 2
    straight = (lane_kind == 0) & (lane_real == row_real)
    crossed = (lane_kind == 1) & (lane_real != row_real)
    cross_sign = jnp.where(row_stokes == row_real, -1.0, 1.0)
    mask = [
        jnp.where(straight & (row_stokes == stokes), 1.0, 0.0)
        + jnp.where(crossed & (row_stokes != stokes), cross_sign, 0.0)
        for stokes in range(2)
    ]

    arrived(recv2, 1)
    sums = [recv2[block] * turned[block] for block in range(blks)]
    step = blks // 2
    while step >= 1:
        upper = (low_lane // step) % 2 == 1
        merged = []
        for block in range(step):
            one, two = sums[block], sums[block + step]
            kept = jnp.where(upper, two, one)
            moved = jnp.where(upper, one, two)
            merged.append(
                kept
                + jnp.where(
                    upper, pltpu.roll(moved, step, 1), pltpu.roll(moved, lanes - step, 1)
                )
            )
        sums = merged
        step //= 2
    total_sum = sums[0]
    odd_part = (iota(total_sum.shape, 1) // blks) % 2 == 1
    total_sum = total_sum + jnp.where(
        odd_part, pltpu.roll(total_sum, blks, 1), pltpu.roll(total_sum, lanes - blks, 1)
    )
    total_sum = total_sum.astype(BF16).astype(F32)
    left = jnp.concatenate(
        [
            mask[0] * total_sum[2 * chan : 2 * chan + 1]
            + mask[1] * total_sum[2 * chan + 1 : 2 * chan + 2]
            for chan in range(chans)
        ],
        axis=0,
    )
    alm_grads = dot(left.astype(BF16), back_leg, NN)
    scaled = [
        alm_grads[8 * chan : 8 * chan + 8] * gain_v[pl.ds(chan, 1), :] for chan in range(chans)
    ]
    for comp in range(comps):
        mixed = mix_s[chan_s[0], comp] * scaled[0]
        for chan in range(1, chans):
            mixed = mixed + mix_s[chan_s[chan], comp] * scaled[chan]
        out_ref[comp] = mixed[0:4]
    sent(recv1, 0)
    sent(recv2, 1)


def body(
    chans, blks, comp_alms, legendre, inv_noise, beam_window, mixing, channel_of, m_orders,
    cycle_of, cycle_pixels,
):
    comps, parts, order_dev, shard = comp_alms.shape
    cycles = legendre.shape[3]
    chan_dev, stokes, slots, width = inv_noise.shape
    assert parts == 4 and stokes == 2 and order_dev == 1 and chan_dev == 1
    lanes = 4 * cycles
    assert slots * blks == cycles
    chunks = width // LANES
    assert 2 * chunks == LANES
    noise = jnp.swapaxes(inv_noise.reshape(stokes, slots, chunks, LANES), 1, 2)
    any_space = pl.BlockSpec(memory_space=pl.ANY)
    vector = pl.BlockSpec(memory_space=pltpu.VMEM)
    result = pl.pallas_call(
        functools.partial(kernel, chans, blks),
        out_shape=pltpu.VMEM((comps, 4, shard), F32),
        in_specs=[any_space] * 10,
        out_specs=vector,
        scratch_shapes=[
            pltpu.SMEM(mixing.shape, F32),
            pltpu.SMEM(channel_of.shape, jnp.int32),
            pltpu.SMEM(m_orders.shape, jnp.int32),
            pltpu.SMEM(cycle_of.shape, jnp.int32),
            pltpu.SMEM(cycle_pixels.shape, jnp.int32),
            pltpu.VMEM((1, cycles), jnp.int32),
            pltpu.VMEM((comps, 8, shard), F32),
            pltpu.VMEM((2, cycles, shard), BF16),
            pltpu.VMEM((slots, 2 * chunks, LANES), F32),
            pltpu.VMEM((beam_window.shape[0], shard), F32),
            pltpu.VMEM((chans, shard), F32),
            pltpu.VMEM((slots, 4 * blks * blks, LANES), BF16),
            pltpu.VMEM((slots, 4 * blks * blks, LANES), F32),
            pltpu.VMEM((chans, lanes), F32),
            pltpu.VMEM((chans, blks, chans, lanes), F32),
            pltpu.VMEM((blks, 2, lanes), F32),
            pltpu.VMEM((blks, 2 * chans, lanes), F32),
            pltpu.VMEM((chans, lanes), F32),
            pltpu.VMEM((2, lanes), F32),
            pltpu.VMEM((blks, lanes // LANES, 2 * chans, LANES), F32),
            pltpu.SemaphoreType.DMA((10,)),
            pltpu.SemaphoreType.DMA((2,)),
            pltpu.SemaphoreType.DMA((2,)),
        ],
        compiler_params=pltpu.CompilerParams(collective_id=0, has_side_effects=True),
        name="normal_product",
    )(
        comp_alms, jnp.swapaxes(legendre, 2, 3), noise, beam_window, mixing, channel_of,
        m_orders, cycle_of, cycle_pixels, cycle_of.reshape(1, cycles),
    )
    return result.reshape(comp_alms.shape)


def solution(mesh):
    in_specs = (
        P(None, None, "blk", "chan"),
        P(None, "blk", None, None),
        P("chan", None, "blk", None),
        P(),
        P(),
        P(),
        P(),
        P(),
        P(),
    )
    out_specs = P(None, None, "blk", "chan")
    work = functools.partial(body, mesh.shape["chan"], mesh.shape["blk"])
    return jax.shard_map(work, mesh=mesh, in_specs=in_specs, out_specs=out_specs, check_vma=False)
```

```python
import functools
import math

import jax
import jax.numpy as jnp
from jax import lax
from jax.experimental import pallas as pl
from jax.experimental.pallas import tpu as pltpu
from jax.sharding import PartitionSpec as P

F32 = jnp.float32
BF16 = jnp.bfloat16
LANES = 128
NT = (((1,), (1,)), ((), ()))
NN = (((1,), (0,)), ((), ()))


def iota(shape, dim):
    return lax.broadcasted_iota(jnp.int32, shape, dim)


def dot(left, right, dims):
    return lax.dot_general(left, right, dims, preferred_element_type=F32)


def rest(value, size):
    return value & (size - 1) if size & (size - 1) == 0 else lax.rem(value, jnp.int32(size))


def share(value, size):
    if size & (size - 1) == 0:
        return value >> (size.bit_length() - 1)
    return lax.div(value, jnp.int32(size))


def turn(steps, count, double_inverse):
    quarter = jnp.floor(steps * double_inverse + 0.5)
    angle = (2.0 * steps - quarter * count) * (double_inverse * jnp.float32(math.pi / 4))
    square = angle * angle
    sine = angle + angle * square * (
        (-1.9515295891e-4 * square + 8.3321608736e-3) * square - 1.6666654611e-1
    )
    cosine = (1.0 - 0.5 * square) + square * square * (
        (2.443315711809948e-5 * square - 1.388731625493765e-3) * square + 4.166664568298827e-2
    )
    index = quarter.astype(jnp.int32)
    odd = (index & 1) == 1
    real = jnp.where(odd, sine, cosine)
    imag = jnp.where(odd, cosine, sine)
    real = jnp.where(((index + 1) & 2) == 2, -real, real)
    imag = jnp.where((index & 2) == 2, -imag, imag)
    return real, imag


def pair_turns(cosines, sines, order):
    cos_one, sin_one = cosines[order : order + 1], sines[order : order + 1]
    cos_cos, sin_sin = cos_one * cosines, sin_one * sines
    sin_cos, cos_sin = sin_one * cosines, cos_one * sines
    return [cos_cos - sin_sin, sin_cos + cos_sin, cos_cos + sin_sin, sin_cos - cos_sin]


def kernel(
    chans, blks, alm_hbm, leg_hbm, inv_hbm, beam_hbm, mix_hbm, chan_hbm, order_hbm, cycle_hbm,
    pixel_hbm, cycle_row_hbm, out_ref, mix_s, chan_s, order_s, cycle_s, pixel_s, cycle_row, comp_v,
    leg_v, inv_v, beam_v, gain_v, fine_v, coarse_v, send1, recv1, send2, recv2, spare1, spare2, twin_v,
    in_sem, send_sem, recv_sem,
):
    comps = comp_v.shape[0]
    shard = comp_v.shape[2]
    cycles = leg_v.shape[1]
    slots = inv_v.shape[0]
    chunks = inv_v.shape[1] // 2
    rows = 4 * chans
    lanes = 4 * cycles
    total = chans * blks
    me_c = lax.axis_index("chan")
    me_b = lax.axis_index("blk")
    first = pl.multiple_of(me_c * shard, shard)

    me = me_b * chans + me_c

    def peer(offset):
        index = offset - 1 + (me < offset).astype(jnp.int32)
        return lax.rem(index, chans), index // chans

    def each(first_offset, last_offset, act):
        if last_offset - first_offset <= 64:
            for offset in range(first_offset, last_offset):
                act(offset)
        else:
            lax.fori_loop(
                first_offset, last_offset, lambda offset, carry: (act(offset), carry)[1], 0
            )

    barrier = pltpu.get_barrier_semaphore()

    def tell(semaphore, dest_c, dest_b):
        pl.semaphore_signal(
            semaphore,
            inc=1,
            device_id=(dest_c, dest_b),
            device_id_type=pl.DeviceIdType.MESH,
        )

    scalars = []

    def load(src, dst, group):
        copy = pltpu.make_async_copy(src, dst, in_sem.at[group])
        copy.start()
        return copy

    def loaded(dst, group):
        pltpu.make_async_copy(dst, dst, in_sem.at[group]).wait()

    for src, dst in (
        (order_hbm, order_s), (cycle_hbm, cycle_s), (pixel_hbm, pixel_s), (mix_hbm, mix_s),
        (chan_hbm, chan_s), (cycle_row_hbm, cycle_row),
    ):
        scalars.append(load(src, dst, 4 + len(scalars)))
    for kind in range(2):
        load(leg_hbm.at[kind, 0, :, pl.ds(first, shard)], leg_v.at[kind], 2)
    for comp in range(comps):
        for part in range(4):
            for half in range(2):
                load(alm_hbm.at[comp, part], comp_v.at[comp, pl.ds(4 * half + part, 1), :], 0)
    load(beam_hbm.at[:, pl.ds(first, shard)], beam_v, 1)
    for stokes in range(2):
        for slot in range(slots):
            load(
                inv_hbm.at[stokes, :, slot, :],
                inv_v.at[slot, pl.ds(stokes * chunks, chunks), :],
                3,
            )
    each(
        1,
        total,
        lambda offset: tell(
            barrier, lax.rem(me_c + offset // blks, chans), lax.rem(me_b + offset % blks, blks)
        ),
    )
    for copy in scalars:
        copy.wait()

    own_cycles = [cycle_s[me_b * slots + slot] for slot in range(slots)]
    own_pixels = [pixel_s[cycle].astype(F32) for cycle in own_cycles]

    def by_slot(slot_index, values):
        result = jnp.where(slot_index == 0, values[0], values[slots - 1])
        for slot in range(1, slots - 1):
            result = jnp.where(slot_index == slot, values[slot], result)
        return result

    grid = (blks, LANES)
    row = iota(grid, 0)
    lane = iota(grid, 1)
    orders = jnp.full(grid, order_s[0], jnp.int32)
    for order in range(1, blks):
        orders = jnp.where(row == order, order_s[order], orders)
    orders = orders.astype(F32)
    fine = orders * (2 * lane + 1).astype(F32)
    leap = orders * (2.0 * LANES)
    chunk = rest(lane, chunks).astype(F32)
    for slot in range(slots):
        pixels = jnp.full(grid, own_pixels[slot], F32)
        reciprocal = 1.0 / pixels
        stride = leap - jnp.floor(leap * (0.5 * reciprocal)) * (2.0 * pixels)
        fine_turn = turn(fine, pixels, 2.0 * reciprocal)
        coarse_turn = turn(stride * chunk, pixels, 2.0 * reciprocal)
        for order in range(blks):
            block = pl.ds(order * 4 * blks, 4 * blks)
            fine_v[slot, block, :] = jnp.concatenate(
                pair_turns(*fine_turn, order), axis=0
            ).astype(BF16)
            coarse_v[slot, block, :] = jnp.concatenate(pair_turns(*coarse_turn, order), axis=0)

    loaded(comp_v, 0)
    loaded(beam_v, 1)
    loaded(leg_v, 2)
    low_half = iota((8, 1), 0) < 4
    keep = (iota((1, shard), 1) + first >= order_s[me_b]).astype(F32)
    alm_rows = []
    for pair in range(chans // 2):
        picked = [chan_s[2 * pair], chan_s[2 * pair + 1]]
        columns = [
            jnp.where(low_half, mix_s[picked[0], comp], mix_s[picked[1], comp])
            for comp in range(comps)
        ]
        mixed = columns[0] * comp_v[0]
        for comp in range(1, comps):
            mixed = mixed + columns[comp] * comp_v[comp]
        gains = [beam_v[pl.ds(chan, 1), :] * keep for chan in picked]
        gain_v[pl.ds(2 * pair, 1), :] = gains[0]
        gain_v[pl.ds(2 * pair + 1, 1), :] = gains[1]
        alm_rows.append(mixed * jnp.where(low_half, gains[0], gains[1]))
    alm = jnp.concatenate(alm_rows, axis=0).astype(BF16)
    plus = dot(alm, jnp.concatenate([leg_v[0]] * 4, axis=0), NT)
    minus = dot(alm, jnp.concatenate([leg_v[1]] * 4, axis=0), NT)
    row_part = iota(plus.shape, 0) % 4
    lane_part = iota(plus.shape, 1) // cycles
    outer = (lane_part == 0) | (lane_part == 3)
    signed = jnp.where(outer, -minus, minus)
    joined = jnp.where(lane_part == row_part, plus, 0.0) + jnp.where(
        lane_part == 3 - row_part, signed, 0.0
    )
    folded = joined
    for step in range(1, 4):
        folded = folded + pltpu.roll(joined, rows - step, 0)
    for chan in range(chans):
        send1[pl.ds(chan, 1), :] = folded[4 * chan : 4 * chan + 1]


    def arrived(dst, phase):
        pltpu.make_async_copy(dst, dst, recv_sem.at[phase]).wait()

    def sent(dst, phase):
        pltpu.make_async_copy(dst, dst, send_sem.at[phase]).wait()

    def routes(dest_b):
        return (
            (send1, recv1.at[me_c, me_b]),
            (send2.at[dest_b], recv2.at[me_b, pl.ds(2 * me_c, 2), :]),
        )

    def post(offset, phase):
        dest_c, dest_b = peer(offset)
        src, dst = routes(dest_b)[phase]
        pltpu.make_async_remote_copy(
            src_ref=src,
            dst_ref=dst,
            send_sem=send_sem.at[phase],
            recv_sem=recv_sem.at[phase],
            device_id=(dest_c, dest_b),
            device_id_type=pl.DeviceIdType.MESH,
        ).start()

    early = min(4, total - 1)
    pl.semaphore_wait(barrier, total - 1)
    each(1, early + 1, lambda offset: post(offset, 0))
    loaded(inv_v, 3)
    grid = (2 * chunks, LANES)
    pixel_index = rest(iota(grid, 0), chunks) * LANES + iota(grid, 1)
    parts = [[] for _ in range(blks)]
    for slot in range(slots):
        live = pixel_index.astype(F32) < own_pixels[slot]
        noise = jnp.where(live, inv_v[slot], 0.0).astype(BF16)
        inner = dot(fine_v[slot], noise, NT)
        for order in range(blks):
            base = order * 4 * blks
            held = [inner[base + kind * blks : base + (kind + 1) * blks] for kind in range(4)]
            outer_turn = [
                coarse_v[slot, pl.ds(base + kind * blks, blks), :] for kind in range(4)
            ]
            add_real = outer_turn[0] * held[0] - outer_turn[1] * held[1]
            add_imag = outer_turn[0] * held[1] + outer_turn[1] * held[0]
            sub_real = outer_turn[2] * held[2] - outer_turn[3] * held[3]
            sub_imag = outer_turn[2] * held[3] + outer_turn[3] * held[2]
            parts[order].append(
                jnp.concatenate(
                    [
                        sub_real + add_real,
                        sub_imag - add_imag,
                        -sub_imag - add_imag,
                        sub_real - add_real,
                    ],
                    axis=0,
                ).astype(BF16)
            )
    ones = (share(iota((8, LANES), 1), chunks) == iota((8, LANES), 0)).astype(F32).astype(BF16)
    weight = 0.5 / by_slot(share(iota((2, lanes), 1), 4 * blks), own_pixels)
    for order in range(blks):
        summed = dot(ones, jnp.concatenate(parts[order], axis=0), NT)
        send2[order] = summed[0:2] * weight
    each(1, early + 1, lambda offset: post(offset, 1))
    each(early + 1, total, lambda offset: (post(offset, 0), post(offset, 1)))
    for phase, (src, dst) in enumerate(routes(me_b)):
        pltpu.make_async_copy(src, dst, recv_sem.at[phase]).start()
        pltpu.make_async_copy(src, (spare1, spare2)[phase], send_sem.at[phase]).start()

    to_lane = iota((cycles, lanes), 1)
    spread = (
        iota((cycles, lanes), 0) == rest(to_lane, blks) * slots + share(to_lane, 4 * blks)
    ).astype(F32).astype(BF16)
    lane_cycle = dot(
        jnp.broadcast_to(cycle_row[...].astype(F32), (8, cycles)).astype(BF16), spread, NN
    )[0:1]
    half = (2 * cycles, lanes)
    from_row = iota(half, 0)
    shuffle = (
        (rest(from_row, cycles).astype(F32) == lane_cycle)
        & (share(from_row, cycles) == (share(iota(half, 1), blks) & 1))
    ).astype(F32)
    leg_stack = jnp.concatenate([leg_v[0], leg_v[1]], axis=0)
    back_leg = dot(shuffle.T.astype(BF16), leg_stack, NN).astype(BF16)
    empty = jnp.zeros(half, F32)
    shuffle = jnp.concatenate(
        [
            jnp.concatenate([shuffle, empty], axis=1),
            jnp.concatenate([empty, shuffle], axis=1),
        ],
        axis=0,
    ).astype(BF16)

    arrived(recv1, 0)
    gathered = []
    for order in range(blks):
        coeffs = recv1[0, order]
        for chan in range(1, chans):
            coeffs = coeffs + recv1[chan, order]
        gathered.append(coeffs)
    coeffs = dot(jnp.concatenate(gathered, axis=0).astype(BF16), shuffle, NN)
    for order in range(blks):
        own = coeffs[order * chans : (order + 1) * chans]
        for tile in range(lanes // LANES):
            for part in range(2):
                begin = part * lanes + tile * LANES
                twin_v[order, tile, pl.ds(part, chans, stride=2), :] = own[
                    :, begin : begin + LANES
                ]
    turned = [
        jnp.concatenate([twin_v[order, tile] for tile in range(lanes // LANES)], axis=1)
        for order in range(blks)
    ]
    low_lane = iota((2 * chans, lanes), 1)
    step = 1
    while step < blks:
        upper = (share(low_lane, step) & 1) == 1
        following = list(turned)
        for order in range(blks):
            if (order // step) % 2 == 0:
                one, two = turned[order], turned[order + step]
                following[order] = jnp.where(upper, pltpu.roll(two, step, 1), one)
                following[order + step] = jnp.where(
                    upper, two, pltpu.roll(one, lanes - step, 1)
                )
        turned = following
        step *= 2

    final_row = iota((8, lanes), 0)
    final_lane = iota((8, lanes), 1)
    row_real = final_row & 1
    row_stokes = (final_row >> 1) & 1
    lane_kind = share(final_lane, blks) & 1
    lane_real = share(final_lane, 2 * blks) & 1
    straight = (lane_kind == 0) & (lane_real == row_real)
    crossed = (lane_kind == 1) & (lane_real != row_real)
    cross_sign = jnp.where(row_stokes == row_real, -1.0, 1.0)
    mask = [
        jnp.where(straight & (row_stokes == stokes), 1.0, 0.0)
        + jnp.where(crossed & (row_stokes != stokes), cross_sign, 0.0)
        for stokes in range(2)
    ]

    arrived(recv2, 1)
    sums = [recv2[block] * turned[block] for block in range(blks)]
    step = blks // 2
    while step >= 1:
        upper = (share(low_lane, step) & 1) == 1
        merged = []
        for block in range(step):
            one, two = sums[block], sums[block + step]
            kept = jnp.where(upper, two, one)
            moved = jnp.where(upper, one, two)
            merged.append(
                kept
                + jnp.where(
                    upper, pltpu.roll(moved, step, 1), pltpu.roll(moved, lanes - step, 1)
                )
            )
        sums = merged
        step //= 2
    total_sum = sums[0]
    odd_part = (share(iota(total_sum.shape, 1), blks) & 1) == 1
    total_sum = total_sum + jnp.where(
        odd_part, pltpu.roll(total_sum, blks, 1), pltpu.roll(total_sum, lanes - blks, 1)
    )
    total_sum = total_sum.astype(BF16).astype(F32)
    left = jnp.concatenate(
        [
            mask[0] * total_sum[2 * chan : 2 * chan + 1]
            + mask[1] * total_sum[2 * chan + 1 : 2 * chan + 2]
            for chan in range(chans)
        ],
        axis=0,
    )
    alm_grads = dot(left.astype(BF16), back_leg, NN)
    scaled = [
        alm_grads[8 * chan : 8 * chan + 8] * gain_v[pl.ds(chan, 1), :] for chan in range(chans)
    ]
    for comp in range(comps):
        mixed = mix_s[chan_s[0], comp] * scaled[0]
        for chan in range(1, chans):
            mixed = mixed + mix_s[chan_s[chan], comp] * scaled[chan]
        out_ref[comp] = mixed[0:4]
    sent(recv1, 0)
    sent(recv2, 1)


def body(
    chans, blks, comp_alms, legendre, inv_noise, beam_window, mixing, channel_of, m_orders,
    cycle_of, cycle_pixels,
):
    comps, parts, order_dev, shard = comp_alms.shape
    cycles = legendre.shape[3]
    chan_dev, stokes, slots, width = inv_noise.shape
    assert parts == 4 and stokes == 2 and order_dev == 1 and chan_dev == 1
    lanes = 4 * cycles
    assert slots * blks == cycles
    chunks = width // LANES
    assert 2 * chunks == LANES
    noise = jnp.swapaxes(inv_noise.reshape(stokes, slots, chunks, LANES), 1, 2)
    any_space = pl.BlockSpec(memory_space=pl.ANY)
    vector = pl.BlockSpec(memory_space=pltpu.VMEM)
    result = pl.pallas_call(
        functools.partial(kernel, chans, blks),
        out_shape=pltpu.VMEM((comps, 4, shard), F32),
        in_specs=[any_space] * 10,
        out_specs=vector,
        scratch_shapes=[
            pltpu.SMEM(mixing.shape, F32),
            pltpu.SMEM(channel_of.shape, jnp.int32),
            pltpu.SMEM(m_orders.shape, jnp.int32),
            pltpu.SMEM(cycle_of.shape, jnp.int32),
            pltpu.SMEM(cycle_pixels.shape, jnp.int32),
            pltpu.VMEM((1, cycles), jnp.int32),
            pltpu.VMEM((comps, 8, shard), F32),
            pltpu.VMEM((2, cycles, shard), BF16),
            pltpu.VMEM((slots, 2 * chunks, LANES), F32),
            pltpu.VMEM((beam_window.shape[0], shard), F32),
            pltpu.VMEM((chans, shard), F32),
            pltpu.VMEM((slots, 4 * blks * blks, LANES), BF16),
            pltpu.VMEM((slots, 4 * blks * blks, LANES), F32),
            pltpu.VMEM((chans, lanes), F32),
            pltpu.VMEM((chans, blks, chans, lanes), F32),
            pltpu.VMEM((blks, 2, lanes), F32),
            pltpu.VMEM((blks, 2 * chans, lanes), F32),
            pltpu.VMEM((chans, lanes), F32),
            pltpu.VMEM((2, lanes), F32),
            pltpu.VMEM((blks, lanes // LANES, 2 * chans, LANES), F32),
            pltpu.SemaphoreType.DMA((10,)),
            pltpu.SemaphoreType.DMA((2,)),
            pltpu.SemaphoreType.DMA((2,)),
        ],
        compiler_params=pltpu.CompilerParams(collective_id=0, has_side_effects=True),
        name="normal_product",
    )(
        comp_alms, jnp.swapaxes(legendre, 2, 3), noise, beam_window, mixing, channel_of,
        m_orders, cycle_of, cycle_pixels, cycle_of.reshape(1, cycles),
    )
    return result.reshape(comp_alms.shape)


def solution(mesh):
    in_specs = (
        P(None, None, "blk", "chan"),
        P(None, "blk", None, None),
        P("chan", None, "blk", None),
        P(),
        P(),
        P(),
        P(),
        P(),
        P(),
    )
    out_specs = P(None, None, "blk", "chan")
    work = functools.partial(body, mesh.shape["chan"], mesh.shape["blk"])
    return jax.shard_map(work, mesh=mesh, in_specs=in_specs, out_specs=out_specs, check_vma=False)
```

```python
import functools
import math

import jax
import jax.numpy as jnp
from jax import lax
from jax.experimental import pallas as pl
from jax.experimental.pallas import tpu as pltpu
from jax.sharding import PartitionSpec as P

F32 = jnp.float32
BF16 = jnp.bfloat16
LANES = 128
NT = (((1,), (1,)), ((), ()))
NN = (((1,), (0,)), ((), ()))


def iota(shape, dim):
    return lax.broadcasted_iota(jnp.int32, shape, dim)


def dot(left, right, dims):
    return lax.dot_general(left, right, dims, preferred_element_type=F32)


def rest(value, size):
    return value & (size - 1) if size & (size - 1) == 0 else lax.rem(value, jnp.int32(size))


def share(value, size):
    if size & (size - 1) == 0:
        return value >> (size.bit_length() - 1)
    return lax.div(value, jnp.int32(size))


def turn(steps, count, double_inverse):
    quarter = jnp.floor(steps * double_inverse + 0.5)
    angle = (2.0 * steps - quarter * count) * (double_inverse * jnp.float32(math.pi / 4))
    square = angle * angle
    sine = angle + angle * square * (
        (-1.9515295891e-4 * square + 8.3321608736e-3) * square - 1.6666654611e-1
    )
    cosine = (1.0 - 0.5 * square) + square * square * (
        (2.443315711809948e-5 * square - 1.388731625493765e-3) * square + 4.166664568298827e-2
    )
    index = quarter.astype(jnp.int32)
    odd = (index & 1) == 1
    real = jnp.where(odd, sine, cosine)
    imag = jnp.where(odd, cosine, sine)
    real = jnp.where(((index + 1) & 2) == 2, -real, real)
    imag = jnp.where((index & 2) == 2, -imag, imag)
    return real, imag


def pair_turns(cosines, sines, order):
    cos_one, sin_one = cosines[order : order + 1], sines[order : order + 1]
    cos_cos, sin_sin = cos_one * cosines, sin_one * sines
    sin_cos, cos_sin = sin_one * cosines, cos_one * sines
    return [cos_cos - sin_sin, sin_cos + cos_sin, cos_cos + sin_sin, sin_cos - cos_sin]


def kernel(
    chans, blks, alm_hbm, leg_hbm, inv_hbm, beam_hbm, mix_hbm, chan_hbm, order_hbm, cycle_hbm,
    pixel_hbm, cycle_row_hbm, out_ref, mix_s, chan_s, order_s, cycle_s, pixel_s, cycle_row, comp_v,
    leg_v, inv_v, beam_v, gain_v, fine_v, coarse_v, send1, recv1, send2, recv2, spare1, spare2, twin_v,
    in_sem, send_sem, recv_sem,
):
    comps = comp_v.shape[0]
    shard = comp_v.shape[2]
    cycles = leg_v.shape[1]
    slots = inv_v.shape[0]
    chunks = inv_v.shape[1] // 2
    rows = 4 * chans
    lanes = 4 * cycles
    total = chans * blks
    me_c = lax.axis_index("chan")
    me_b = lax.axis_index("blk")
    first = pl.multiple_of(me_c * shard, shard)

    me = me_b * chans + me_c

    def peer(offset):
        index = offset - 1 + (me < offset).astype(jnp.int32)
        return rest(index, chans), share(index, chans)

    def each(first_offset, last_offset, act):
        if last_offset - first_offset <= 64:
            for offset in range(first_offset, last_offset):
                act(offset)
        else:
            lax.fori_loop(
                first_offset, last_offset, lambda offset, carry: (act(offset), carry)[1], 0
            )

    barrier = pltpu.get_barrier_semaphore()

    def tell(semaphore, dest_c, dest_b):
        pl.semaphore_signal(
            semaphore,
            inc=1,
            device_id=(dest_c, dest_b),
            device_id_type=pl.DeviceIdType.MESH,
        )

    scalars = []

    def load(src, dst, group):
        copy = pltpu.make_async_copy(src, dst, in_sem.at[group])
        copy.start()
        return copy

    def loaded(dst, group):
        pltpu.make_async_copy(dst, dst, in_sem.at[group]).wait()

    for src, dst in (
        (order_hbm, order_s), (cycle_hbm, cycle_s), (pixel_hbm, pixel_s), (mix_hbm, mix_s),
        (chan_hbm, chan_s), (cycle_row_hbm, cycle_row),
    ):
        scalars.append(load(src, dst, 4 + len(scalars)))
    for kind in range(2):
        load(leg_hbm.at[kind, 0, :, pl.ds(first, shard)], leg_v.at[kind], 2)
    for comp in range(comps):
        for half in range(2):
            load(alm_hbm.at[comp, :, 0, :], comp_v.at[comp, pl.ds(4 * half, 4), :], 0)
    load(beam_hbm.at[:, pl.ds(first, shard)], beam_v, 1)
    for stokes in range(2):
        for slot in range(slots):
            load(
                inv_hbm.at[stokes, :, slot, :],
                inv_v.at[slot, pl.ds(stokes * chunks, chunks), :],
                3,
            )
    each(
        1,
        total,
        lambda offset: tell(
            barrier, rest(me_c + offset // blks, chans), rest(me_b + offset % blks, blks)
        ),
    )
    for copy in scalars:
        copy.wait()

    own_cycles = [cycle_s[me_b * slots + slot] for slot in range(slots)]
    own_pixels = [pixel_s[cycle].astype(F32) for cycle in own_cycles]

    def by_slot(slot_index, values):
        result = jnp.where(slot_index == 0, values[0], values[slots - 1])
        for slot in range(1, slots - 1):
            result = jnp.where(slot_index == slot, values[slot], result)
        return result

    grid = (blks, LANES)
    row = iota(grid, 0)
    lane = iota(grid, 1)
    orders = jnp.full(grid, order_s[0], jnp.int32)
    for order in range(1, blks):
        orders = jnp.where(row == order, order_s[order], orders)
    orders = orders.astype(F32)
    fine = orders * (2 * lane + 1).astype(F32)
    leap = orders * (2.0 * LANES)
    chunk = rest(lane, chunks).astype(F32)
    def table(slot):
        pixels = jnp.full(grid, own_pixels[slot], F32)
        reciprocal = 1.0 / pixels
        stride = leap - jnp.floor(leap * (0.5 * reciprocal)) * (2.0 * pixels)
        fine_turn = turn(fine, pixels, 2.0 * reciprocal)
        coarse_turn = turn(stride * chunk, pixels, 2.0 * reciprocal)
        for order in range(blks):
            block = pl.ds(order * 4 * blks, 4 * blks)
            fine_v[slot, block, :] = jnp.concatenate(
                pair_turns(*fine_turn, order), axis=0
            ).astype(BF16)
            coarse_v[slot, block, :] = jnp.concatenate(pair_turns(*coarse_turn, order), axis=0)

    for slot in range(3):
        table(slot)
    loaded(comp_v, 0)
    loaded(beam_v, 1)
    loaded(leg_v, 2)
    for slot in range(3, slots):
        table(slot)

    low_half = iota((8, 1), 0) < 4
    keep = (iota((1, shard), 1) + first >= order_s[me_b]).astype(F32)
    alm_rows = []
    for pair in range(chans // 2):
        picked = [chan_s[2 * pair], chan_s[2 * pair + 1]]
        columns = [
            jnp.where(low_half, mix_s[picked[0], comp], mix_s[picked[1], comp])
            for comp in range(comps)
        ]
        mixed = columns[0] * comp_v[0]
        for comp in range(1, comps):
            mixed = mixed + columns[comp] * comp_v[comp]
        gains = [beam_v[pl.ds(chan, 1), :] * keep for chan in picked]
        gain_v[pl.ds(2 * pair, 1), :] = gains[0]
        gain_v[pl.ds(2 * pair + 1, 1), :] = gains[1]
        alm_rows.append(mixed * jnp.where(low_half, gains[0], gains[1]))
    alm = jnp.concatenate(alm_rows, axis=0).astype(BF16)
    plus = dot(alm, jnp.concatenate([leg_v[0]] * 4, axis=0), NT)
    minus = dot(alm, jnp.concatenate([leg_v[1]] * 4, axis=0), NT)
    row_part = iota(plus.shape, 0) % 4
    lane_part = iota(plus.shape, 1) // cycles
    outer = (lane_part == 0) | (lane_part == 3)
    signed = jnp.where(outer, -minus, minus)
    joined = jnp.where(lane_part == row_part, plus, 0.0) + jnp.where(
        lane_part == 3 - row_part, signed, 0.0
    )
    folded = joined
    for step in range(1, 4):
        folded = folded + pltpu.roll(joined, rows - step, 0)
    for chan in range(chans):
        send1[pl.ds(chan, 1), :] = folded[4 * chan : 4 * chan + 1]


    def arrived(dst, phase):
        pltpu.make_async_copy(dst, dst, recv_sem.at[phase]).wait()

    def sent(dst, phase):
        pltpu.make_async_copy(dst, dst, send_sem.at[phase]).wait()

    def routes(dest_b):
        return (
            (send1, recv1.at[me_c, me_b]),
            (send2.at[dest_b], recv2.at[me_b, pl.ds(2 * me_c, 2), :]),
        )

    def post(offset, phase):
        dest_c, dest_b = peer(offset)
        src, dst = routes(dest_b)[phase]
        pltpu.make_async_remote_copy(
            src_ref=src,
            dst_ref=dst,
            send_sem=send_sem.at[phase],
            recv_sem=recv_sem.at[phase],
            device_id=(dest_c, dest_b),
            device_id_type=pl.DeviceIdType.MESH,
        ).start()

    early = min(4, total - 1)
    pl.semaphore_wait(barrier, total - 1)
    each(1, early + 1, lambda offset: post(offset, 0))
    loaded(inv_v, 3)
    grid = (2 * chunks, LANES)
    pixel_index = rest(iota(grid, 0), chunks) * LANES + iota(grid, 1)
    parts = [[] for _ in range(blks)]
    for slot in range(slots):
        live = pixel_index.astype(F32) < own_pixels[slot]
        noise = jnp.where(live, inv_v[slot], 0.0).astype(BF16)
        inner = dot(fine_v[slot], noise, NT)
        for order in range(blks):
            base = order * 4 * blks
            held = [inner[base + kind * blks : base + (kind + 1) * blks] for kind in range(4)]
            outer_turn = [
                coarse_v[slot, pl.ds(base + kind * blks, blks), :] for kind in range(4)
            ]
            add_real = outer_turn[0] * held[0] - outer_turn[1] * held[1]
            add_imag = outer_turn[0] * held[1] + outer_turn[1] * held[0]
            sub_real = outer_turn[2] * held[2] - outer_turn[3] * held[3]
            sub_imag = outer_turn[2] * held[3] + outer_turn[3] * held[2]
            parts[order].append(
                jnp.concatenate(
                    [
                        sub_real + add_real,
                        sub_imag - add_imag,
                        -sub_imag - add_imag,
                        sub_real - add_real,
                    ],
                    axis=0,
                ).astype(BF16)
            )
    ones = (share(iota((8, LANES), 1), chunks) == iota((8, LANES), 0)).astype(F32).astype(BF16)
    weight = 0.5 / by_slot(share(iota((2, lanes), 1), 4 * blks), own_pixels)
    for order in range(blks):
        summed = dot(ones, jnp.concatenate(parts[order], axis=0), NT)
        send2[order] = summed[0:2] * weight
    each(1, early + 1, lambda offset: post(offset, 1))
    each(early + 1, total, lambda offset: (post(offset, 0), post(offset, 1)))
    for phase, (src, dst) in enumerate(routes(me_b)):
        pltpu.make_async_copy(src, dst, recv_sem.at[phase]).start()
        pltpu.make_async_copy(src, (spare1, spare2)[phase], send_sem.at[phase]).start()

    to_lane = iota((cycles, lanes), 1)
    spread = (
        iota((cycles, lanes), 0) == rest(to_lane, blks) * slots + share(to_lane, 4 * blks)
    ).astype(F32).astype(BF16)
    lane_cycle = dot(
        jnp.broadcast_to(cycle_row[...].astype(F32), (8, cycles)).astype(BF16), spread, NN
    )[0:1]
    half = (2 * cycles, lanes)
    from_row = iota(half, 0)
    shuffle = (
        (rest(from_row, cycles).astype(F32) == lane_cycle)
        & (share(from_row, cycles) == (share(iota(half, 1), blks) & 1))
    ).astype(F32)
    leg_stack = jnp.concatenate([leg_v[0], leg_v[1]], axis=0)
    back_leg = dot(shuffle.T.astype(BF16), leg_stack, NN).astype(BF16)
    empty = jnp.zeros(half, F32)
    shuffle = jnp.concatenate(
        [
            jnp.concatenate([shuffle, empty], axis=1),
            jnp.concatenate([empty, shuffle], axis=1),
        ],
        axis=0,
    ).astype(BF16)

    arrived(recv1, 0)
    gathered = []
    for order in range(blks):
        coeffs = recv1[0, order]
        for chan in range(1, chans):
            coeffs = coeffs + recv1[chan, order]
        gathered.append(coeffs)
    coeffs = dot(jnp.concatenate(gathered, axis=0).astype(BF16), shuffle, NN)
    for order in range(blks):
        own = coeffs[order * chans : (order + 1) * chans]
        for tile in range(lanes // LANES):
            for part in range(2):
                begin = part * lanes + tile * LANES
                twin_v[order, tile, pl.ds(part, chans, stride=2), :] = own[
                    :, begin : begin + LANES
                ]
    turned = [
        jnp.concatenate([twin_v[order, tile] for tile in range(lanes // LANES)], axis=1)
        for order in range(blks)
    ]
    low_lane = iota((2 * chans, lanes), 1)
    step = 1
    while step < blks:
        upper = (share(low_lane, step) & 1) == 1
        following = list(turned)
        for order in range(blks):
            if (order // step) % 2 == 0:
                one, two = turned[order], turned[order + step]
                following[order] = jnp.where(upper, pltpu.roll(two, step, 1), one)
                following[order + step] = jnp.where(
                    upper, two, pltpu.roll(one, lanes - step, 1)
                )
        turned = following
        step *= 2

    final_row = iota((8, lanes), 0)
    final_lane = iota((8, lanes), 1)
    row_real = final_row & 1
    row_stokes = (final_row >> 1) & 1
    lane_kind = share(final_lane, blks) & 1
    lane_real = share(final_lane, 2 * blks) & 1
    straight = (lane_kind == 0) & (lane_real == row_real)
    crossed = (lane_kind == 1) & (lane_real != row_real)
    cross_sign = jnp.where(row_stokes == row_real, -1.0, 1.0)
    mask = [
        jnp.where(straight & (row_stokes == stokes), 1.0, 0.0)
        + jnp.where(crossed & (row_stokes != stokes), cross_sign, 0.0)
        for stokes in range(2)
    ]

    arrived(recv2, 1)
    sums = [recv2[block] * turned[block] for block in range(blks)]
    step = blks // 2
    while step >= 1:
        upper = (share(low_lane, step) & 1) == 1
        merged = []
        for block in range(step):
            one, two = sums[block], sums[block + step]
            kept = jnp.where(upper, two, one)
            moved = jnp.where(upper, one, two)
            merged.append(
                kept
                + jnp.where(
                    upper, pltpu.roll(moved, step, 1), pltpu.roll(moved, lanes - step, 1)
                )
            )
        sums = merged
        step //= 2
    total_sum = sums[0]
    odd_part = (share(iota(total_sum.shape, 1), blks) & 1) == 1
    total_sum = total_sum + jnp.where(
        odd_part, pltpu.roll(total_sum, blks, 1), pltpu.roll(total_sum, lanes - blks, 1)
    )
    total_sum = total_sum.astype(BF16).astype(F32)
    left = jnp.concatenate(
        [
            mask[0] * total_sum[2 * chan : 2 * chan + 1]
            + mask[1] * total_sum[2 * chan + 1 : 2 * chan + 2]
            for chan in range(chans)
        ],
        axis=0,
    )
    alm_grads = dot(left.astype(BF16), back_leg, NN)
    scaled = [
        alm_grads[8 * chan : 8 * chan + 8] * gain_v[pl.ds(chan, 1), :] for chan in range(chans)
    ]
    for comp in range(comps):
        mixed = mix_s[chan_s[0], comp] * scaled[0]
        for chan in range(1, chans):
            mixed = mixed + mix_s[chan_s[chan], comp] * scaled[chan]
        out_ref[comp] = mixed[0:4]
    sent(recv1, 0)
    sent(recv2, 1)


def body(
    chans, blks, comp_alms, legendre, inv_noise, beam_window, mixing, channel_of, m_orders,
    cycle_of, cycle_pixels,
):
    comps, parts, order_dev, shard = comp_alms.shape
    cycles = legendre.shape[3]
    chan_dev, stokes, slots, width = inv_noise.shape
    assert parts == 4 and stokes == 2 and order_dev == 1 and chan_dev == 1
    lanes = 4 * cycles
    assert slots * blks == cycles
    chunks = width // LANES
    assert 2 * chunks == LANES
    noise = jnp.swapaxes(inv_noise.reshape(stokes, slots, chunks, LANES), 1, 2)
    any_space = pl.BlockSpec(memory_space=pl.ANY)
    vector = pl.BlockSpec(memory_space=pltpu.VMEM)
    result = pl.pallas_call(
        functools.partial(kernel, chans, blks),
        out_shape=pltpu.VMEM((comps, 4, shard), F32),
        in_specs=[any_space] * 10,
        out_specs=vector,
        scratch_shapes=[
            pltpu.SMEM(mixing.shape, F32),
            pltpu.SMEM(channel_of.shape, jnp.int32),
            pltpu.SMEM(m_orders.shape, jnp.int32),
            pltpu.SMEM(cycle_of.shape, jnp.int32),
            pltpu.SMEM(cycle_pixels.shape, jnp.int32),
            pltpu.VMEM((1, cycles), jnp.int32),
            pltpu.VMEM((comps, 8, shard), F32),
            pltpu.VMEM((2, cycles, shard), BF16),
            pltpu.VMEM((slots, 2 * chunks, LANES), F32),
            pltpu.VMEM((beam_window.shape[0], shard), F32),
            pltpu.VMEM((chans, shard), F32),
            pltpu.VMEM((slots, 4 * blks * blks, LANES), BF16),
            pltpu.VMEM((slots, 4 * blks * blks, LANES), F32),
            pltpu.VMEM((chans, lanes), F32),
            pltpu.VMEM((chans, blks, chans, lanes), F32),
            pltpu.VMEM((blks, 2, lanes), F32),
            pltpu.VMEM((blks, 2 * chans, lanes), F32),
            pltpu.VMEM((chans, lanes), F32),
            pltpu.VMEM((2, lanes), F32),
            pltpu.VMEM((blks, lanes // LANES, 2 * chans, LANES), F32),
            pltpu.SemaphoreType.DMA((10,)),
            pltpu.SemaphoreType.DMA((2,)),
            pltpu.SemaphoreType.DMA((2,)),
        ],
        compiler_params=pltpu.CompilerParams(collective_id=0, has_side_effects=True),
        name="normal_product",
    )(
        comp_alms, jnp.swapaxes(legendre, 2, 3), noise, beam_window, mixing, channel_of,
        m_orders, cycle_of, cycle_pixels, cycle_of.reshape(1, cycles),
    )
    return result.reshape(comp_alms.shape)


def solution(mesh):
    in_specs = (
        P(None, None, "blk", "chan"),
        P(None, "blk", None, None),
        P("chan", None, "blk", None),
        P(),
        P(),
        P(),
        P(),
        P(),
        P(),
    )
    out_specs = P(None, None, "blk", "chan")
    work = functools.partial(body, mesh.shape["chan"], mesh.shape["blk"])
    return jax.shard_map(work, mesh=mesh, in_specs=in_specs, out_specs=out_specs, check_vma=False)
```

```python
import functools
import math

import jax
import jax.numpy as jnp
from jax import lax
from jax.experimental import pallas as pl
from jax.experimental.pallas import tpu as pltpu
from jax.sharding import PartitionSpec as P

F32 = jnp.float32
BF16 = jnp.bfloat16
LANES = 128
NT = (((1,), (1,)), ((), ()))
NN = (((1,), (0,)), ((), ()))


def iota(shape, dim):
    return lax.broadcasted_iota(jnp.int32, shape, dim)


def dot(left, right, dims):
    return lax.dot_general(left, right, dims, preferred_element_type=F32)


def rest(value, size):
    return value & (size - 1) if size & (size - 1) == 0 else lax.rem(value, jnp.int32(size))


def share(value, size):
    if size & (size - 1) == 0:
        return value >> (size.bit_length() - 1)
    return lax.div(value, jnp.int32(size))


def turn(steps, count, double_inverse):
    quarter = jnp.floor(steps * double_inverse + 0.5)
    angle = (2.0 * steps - quarter * count) * (double_inverse * jnp.float32(math.pi / 4))
    square = angle * angle
    sine = angle + angle * square * (
        (-1.9515295891e-4 * square + 8.3321608736e-3) * square - 1.6666654611e-1
    )
    cosine = (1.0 - 0.5 * square) + square * square * (
        (2.443315711809948e-5 * square - 1.388731625493765e-3) * square + 4.166664568298827e-2
    )
    index = quarter.astype(jnp.int32)
    odd = (index & 1) == 1
    real = jnp.where(odd, sine, cosine)
    imag = jnp.where(odd, cosine, sine)
    real = jnp.where(((index + 1) & 2) == 2, -real, real)
    imag = jnp.where((index & 2) == 2, -imag, imag)
    return real, imag


def pair_turns(cosines, sines, order):
    cos_one, sin_one = cosines[order : order + 1], sines[order : order + 1]
    cos_cos, sin_sin = cos_one * cosines, sin_one * sines
    sin_cos, cos_sin = sin_one * cosines, cos_one * sines
    return [cos_cos - sin_sin, sin_cos + cos_sin, cos_cos + sin_sin, sin_cos - cos_sin]


def kernel(
    chans, blks, alm_hbm, leg_hbm, inv_hbm, beam_hbm, mix_hbm, chan_hbm, order_hbm, cycle_hbm,
    pixel_hbm, cycle_row_hbm, out_ref, mix_s, chan_s, order_s, cycle_s, pixel_s, cycle_row, comp_v,
    leg_v, inv_v, beam_v, gain_v, fine_v, coarse_v, send1, recv1, send2, recv2, spare1, spare2, twin_v,
    in_sem, send_sem, recv_sem,
):
    comps = comp_v.shape[0]
    shard = comp_v.shape[2]
    cycles = leg_v.shape[1]
    slots = inv_v.shape[0]
    chunks = inv_v.shape[1] // 2
    rows = 4 * chans
    lanes = 4 * cycles
    total = chans * blks
    me_c = lax.axis_index("chan")
    me_b = lax.axis_index("blk")
    first = pl.multiple_of(me_c * shard, shard)

    me = me_b * chans + me_c

    def peer(offset):
        index = offset - 1 + (me < offset).astype(jnp.int32)
        return rest(index, chans), share(index, chans)

    def each(first_offset, last_offset, act):
        if last_offset - first_offset <= 64:
            for offset in range(first_offset, last_offset):
                act(offset)
        else:
            lax.fori_loop(
                first_offset, last_offset, lambda offset, carry: (act(offset), carry)[1], 0
            )

    barrier = pltpu.get_barrier_semaphore()

    def tell(semaphore, dest_c, dest_b):
        pl.semaphore_signal(
            semaphore,
            inc=1,
            device_id=(dest_c, dest_b),
            device_id_type=pl.DeviceIdType.MESH,
        )

    scalars = []

    def load(src, dst, group):
        copy = pltpu.make_async_copy(src, dst, in_sem.at[group])
        copy.start()
        return copy

    def loaded(dst, group):
        pltpu.make_async_copy(dst, dst, in_sem.at[group]).wait()

    for src, dst in (
        (order_hbm, order_s), (cycle_hbm, cycle_s), (pixel_hbm, pixel_s), (mix_hbm, mix_s),
        (chan_hbm, chan_s), (cycle_row_hbm, cycle_row),
    ):
        scalars.append(load(src, dst, 4 + len(scalars)))
    for kind in range(2):
        load(leg_hbm.at[kind, 0, :, pl.ds(first, shard)], leg_v.at[kind], 2)
    for comp in range(comps):
        for half in range(2):
            load(alm_hbm.at[comp, :, 0, :], comp_v.at[comp, pl.ds(4 * half, 4), :], 0)
    load(beam_hbm.at[:, pl.ds(first, shard)], beam_v, 1)
    for stokes in range(2):
        for slot in range(slots):
            load(
                inv_hbm.at[stokes, :, slot, :],
                inv_v.at[slot, pl.ds(stokes * chunks, chunks), :],
                3,
            )
    each(
        1,
        total,
        lambda offset: tell(
            barrier, rest(me_c + offset // blks, chans), rest(me_b + offset % blks, blks)
        ),
    )
    for copy in scalars:
        copy.wait()

    own_cycles = [cycle_s[me_b * slots + slot] for slot in range(slots)]
    own_pixels = [pixel_s[cycle].astype(F32) for cycle in own_cycles]

    def by_slot(slot_index, values):
        result = jnp.where(slot_index == 0, values[0], values[slots - 1])
        for slot in range(1, slots - 1):
            result = jnp.where(slot_index == slot, values[slot], result)
        return result

    grid = (blks, LANES)
    row = iota(grid, 0)
    lane = iota(grid, 1)
    orders = jnp.full(grid, order_s[0], jnp.int32)
    for order in range(1, blks):
        orders = jnp.where(row == order, order_s[order], orders)
    orders = orders.astype(F32)
    fine = orders * (2 * lane + 1).astype(F32)
    leap = orders * (2.0 * LANES)
    chunk = rest(lane, chunks).astype(F32)
    def table(slot):
        pixels = jnp.full(grid, own_pixels[slot], F32)
        reciprocal = 1.0 / pixels
        stride = leap - jnp.floor(leap * (0.5 * reciprocal)) * (2.0 * pixels)
        fine_turn = turn(fine, pixels, 2.0 * reciprocal)
        short = pixels <= float(LANES)
        fine_turn = [
            jnp.where(short, value.astype(BF16).astype(F32), value) for value in fine_turn
        ]
        coarse_turn = turn(stride * chunk, pixels, 2.0 * reciprocal)
        for order in range(blks):
            block = pl.ds(order * 4 * blks, 4 * blks)
            fine_v[slot, block, :] = jnp.concatenate(
                pair_turns(*fine_turn, order), axis=0
            ).astype(BF16)
            coarse_v[slot, block, :] = jnp.concatenate(pair_turns(*coarse_turn, order), axis=0)

    for slot in range(3):
        table(slot)
    loaded(comp_v, 0)
    loaded(beam_v, 1)
    loaded(leg_v, 2)
    for slot in range(3, slots):
        table(slot)

    low_half = iota((8, 1), 0) < 4
    keep = (iota((1, shard), 1) + first >= order_s[me_b]).astype(F32)
    alm_rows = []
    for pair in range(chans // 2):
        picked = [chan_s[2 * pair], chan_s[2 * pair + 1]]
        columns = [
            jnp.where(low_half, mix_s[picked[0], comp], mix_s[picked[1], comp])
            for comp in range(comps)
        ]
        mixed = columns[0] * comp_v[0]
        for comp in range(1, comps):
            mixed = mixed + columns[comp] * comp_v[comp]
        gains = [beam_v[pl.ds(chan, 1), :] * keep for chan in picked]
        gain_v[pl.ds(2 * pair, 1), :] = gains[0]
        gain_v[pl.ds(2 * pair + 1, 1), :] = gains[1]
        alm_rows.append(mixed * jnp.where(low_half, gains[0], gains[1]))
    alm = jnp.concatenate(alm_rows, axis=0).astype(BF16)
    plus = dot(alm, jnp.concatenate([leg_v[0]] * 4, axis=0), NT)
    minus = dot(alm, jnp.concatenate([leg_v[1]] * 4, axis=0), NT)
    row_part = iota(plus.shape, 0) % 4
    lane_part = iota(plus.shape, 1) // cycles
    outer = (lane_part == 0) | (lane_part == 3)
    signed = jnp.where(outer, -minus, minus)
    joined = jnp.where(lane_part == row_part, plus, 0.0) + jnp.where(
        lane_part == 3 - row_part, signed, 0.0
    )
    folded = joined
    for step in range(1, 4):
        folded = folded + pltpu.roll(joined, rows - step, 0)
    for chan in range(chans):
        send1[pl.ds(chan, 1), :] = folded[4 * chan : 4 * chan + 1]


    def arrived(dst, phase):
        pltpu.make_async_copy(dst, dst, recv_sem.at[phase]).wait()

    def sent(dst, phase):
        pltpu.make_async_copy(dst, dst, send_sem.at[phase]).wait()

    def routes(dest_b):
        return (
            (send1, recv1.at[me_c, me_b]),
            (send2.at[dest_b], recv2.at[me_b, pl.ds(2 * me_c, 2), :]),
        )

    def post(offset, phase):
        dest_c, dest_b = peer(offset)
        src, dst = routes(dest_b)[phase]
        pltpu.make_async_remote_copy(
            src_ref=src,
            dst_ref=dst,
            send_sem=send_sem.at[phase],
            recv_sem=recv_sem.at[phase],
            device_id=(dest_c, dest_b),
            device_id_type=pl.DeviceIdType.MESH,
        ).start()

    early = min(4, total - 1)
    pl.semaphore_wait(barrier, total - 1)
    each(1, early + 1, lambda offset: post(offset, 0))
    loaded(inv_v, 3)
    grid = (2 * chunks, LANES)
    pixel_index = rest(iota(grid, 0), chunks) * LANES + iota(grid, 1)
    parts = [[] for _ in range(blks)]
    for slot in range(slots):
        live = pixel_index.astype(F32) < own_pixels[slot]
        noise = jnp.where(live, inv_v[slot], 0.0).astype(BF16)
        inner = dot(fine_v[slot], noise, NT)
        for order in range(blks):
            base = order * 4 * blks
            held = [inner[base + kind * blks : base + (kind + 1) * blks] for kind in range(4)]
            outer_turn = [
                coarse_v[slot, pl.ds(base + kind * blks, blks), :] for kind in range(4)
            ]
            add_real = outer_turn[0] * held[0] - outer_turn[1] * held[1]
            add_imag = outer_turn[0] * held[1] + outer_turn[1] * held[0]
            sub_real = outer_turn[2] * held[2] - outer_turn[3] * held[3]
            sub_imag = outer_turn[2] * held[3] + outer_turn[3] * held[2]
            blocks = jnp.concatenate(
                [
                    sub_real + add_real,
                    sub_imag - add_imag,
                    -sub_imag - add_imag,
                    sub_real - add_real,
                ],
                axis=0,
            )
            high = blocks.astype(BF16)
            parts[order].append((high, (blocks - high.astype(F32)).astype(BF16)))
    ones = (share(iota((8, LANES), 1), chunks) == iota((8, LANES), 0)).astype(F32).astype(BF16)
    weight = 0.5 / by_slot(share(iota((2, lanes), 1), 4 * blks), own_pixels)
    for order in range(blks):
        summed = dot(ones, jnp.concatenate([high for high, _ in parts[order]], axis=0), NT)
        summed += dot(ones, jnp.concatenate([low for _, low in parts[order]], axis=0), NT)
        send2[order] = summed[0:2] * weight
    each(1, early + 1, lambda offset: post(offset, 1))
    each(early + 1, total, lambda offset: (post(offset, 0), post(offset, 1)))
    for phase, (src, dst) in enumerate(routes(me_b)):
        pltpu.make_async_copy(src, dst, recv_sem.at[phase]).start()
        pltpu.make_async_copy(src, (spare1, spare2)[phase], send_sem.at[phase]).start()

    to_lane = iota((cycles, lanes), 1)
    spread = (
        iota((cycles, lanes), 0) == rest(to_lane, blks) * slots + share(to_lane, 4 * blks)
    ).astype(F32).astype(BF16)
    lane_cycle = dot(
        jnp.broadcast_to(cycle_row[...].astype(F32), (8, cycles)).astype(BF16), spread, NN
    )[0:1]
    half = (2 * cycles, lanes)
    from_row = iota(half, 0)
    shuffle = (
        (rest(from_row, cycles).astype(F32) == lane_cycle)
        & (share(from_row, cycles) == (share(iota(half, 1), blks) & 1))
    ).astype(F32)
    leg_stack = jnp.concatenate([leg_v[0], leg_v[1]], axis=0)
    back_leg = dot(shuffle.T.astype(BF16), leg_stack, NN).astype(BF16)
    empty = jnp.zeros(half, F32)
    shuffle = jnp.concatenate(
        [
            jnp.concatenate([shuffle, empty], axis=1),
            jnp.concatenate([empty, shuffle], axis=1),
        ],
        axis=0,
    ).astype(BF16)

    arrived(recv1, 0)
    gathered = []
    for order in range(blks):
        coeffs = recv1[0, order]
        for chan in range(1, chans):
            coeffs = coeffs + recv1[chan, order]
        gathered.append(coeffs)
    coeffs = dot(jnp.concatenate(gathered, axis=0).astype(BF16), shuffle, NN)
    for order in range(blks):
        own = coeffs[order * chans : (order + 1) * chans]
        for tile in range(lanes // LANES):
            for part in range(2):
                begin = part * lanes + tile * LANES
                twin_v[order, tile, pl.ds(part, chans, stride=2), :] = own[
                    :, begin : begin + LANES
                ]
    turned = [
        jnp.concatenate([twin_v[order, tile] for tile in range(lanes // LANES)], axis=1)
        for order in range(blks)
    ]
    low_lane = iota((2 * chans, lanes), 1)
    step = 1
    while step < blks:
        upper = (share(low_lane, step) & 1) == 1
        following = list(turned)
        for order in range(blks):
            if (order // step) % 2 == 0:
                one, two = turned[order], turned[order + step]
                following[order] = jnp.where(upper, pltpu.roll(two, step, 1), one)
                following[order + step] = jnp.where(
                    upper, two, pltpu.roll(one, lanes - step, 1)
                )
        turned = following
        step *= 2

    final_row = iota((8, lanes), 0)
    final_lane = iota((8, lanes), 1)
    row_real = final_row & 1
    row_stokes = (final_row >> 1) & 1
    lane_kind = share(final_lane, blks) & 1
    lane_real = share(final_lane, 2 * blks) & 1
    straight = (lane_kind == 0) & (lane_real == row_real)
    crossed = (lane_kind == 1) & (lane_real != row_real)
    cross_sign = jnp.where(row_stokes == row_real, -1.0, 1.0)
    mask = [
        jnp.where(straight & (row_stokes == stokes), 1.0, 0.0)
        + jnp.where(crossed & (row_stokes != stokes), cross_sign, 0.0)
        for stokes in range(2)
    ]

    arrived(recv2, 1)
    sums = [recv2[block] * turned[block] for block in range(blks)]
    step = blks // 2
    while step >= 1:
        upper = (share(low_lane, step) & 1) == 1
        merged = []
        for block in range(step):
            one, two = sums[block], sums[block + step]
            kept = jnp.where(upper, two, one)
            moved = jnp.where(upper, one, two)
            merged.append(
                kept
                + jnp.where(
                    upper, pltpu.roll(moved, step, 1), pltpu.roll(moved, lanes - step, 1)
                )
            )
        sums = merged
        step //= 2
    total_sum = sums[0]
    odd_part = (share(iota(total_sum.shape, 1), blks) & 1) == 1
    total_sum = total_sum + jnp.where(
        odd_part, pltpu.roll(total_sum, blks, 1), pltpu.roll(total_sum, lanes - blks, 1)
    )
    total_sum = total_sum.astype(BF16).astype(F32)
    left = jnp.concatenate(
        [
            mask[0] * total_sum[2 * chan : 2 * chan + 1]
            + mask[1] * total_sum[2 * chan + 1 : 2 * chan + 2]
            for chan in range(chans)
        ],
        axis=0,
    )
    alm_grads = dot(left.astype(BF16), back_leg, NN)
    scaled = [
        alm_grads[8 * chan : 8 * chan + 8] * gain_v[pl.ds(chan, 1), :] for chan in range(chans)
    ]
    for comp in range(comps):
        mixed = mix_s[chan_s[0], comp] * scaled[0]
        for chan in range(1, chans):
            mixed = mixed + mix_s[chan_s[chan], comp] * scaled[chan]
        out_ref[comp] = mixed[0:4]
    sent(recv1, 0)
    sent(recv2, 1)


def body(
    chans, blks, comp_alms, legendre, inv_noise, beam_window, mixing, channel_of, m_orders,
    cycle_of, cycle_pixels,
):
    comps, parts, order_dev, shard = comp_alms.shape
    cycles = legendre.shape[3]
    chan_dev, stokes, slots, width = inv_noise.shape
    assert parts == 4 and stokes == 2 and order_dev == 1 and chan_dev == 1
    lanes = 4 * cycles
    assert slots * blks == cycles
    chunks = width // LANES
    assert 2 * chunks == LANES
    noise = jnp.swapaxes(inv_noise.reshape(stokes, slots, chunks, LANES), 1, 2)
    any_space = pl.BlockSpec(memory_space=pl.ANY)
    vector = pl.BlockSpec(memory_space=pltpu.VMEM)
    result = pl.pallas_call(
        functools.partial(kernel, chans, blks),
        out_shape=pltpu.VMEM((comps, 4, shard), F32),
        in_specs=[any_space] * 10,
        out_specs=vector,
        scratch_shapes=[
            pltpu.SMEM(mixing.shape, F32),
            pltpu.SMEM(channel_of.shape, jnp.int32),
            pltpu.SMEM(m_orders.shape, jnp.int32),
            pltpu.SMEM(cycle_of.shape, jnp.int32),
            pltpu.SMEM(cycle_pixels.shape, jnp.int32),
            pltpu.VMEM((1, cycles), jnp.int32),
            pltpu.VMEM((comps, 8, shard), F32),
            pltpu.VMEM((2, cycles, shard), BF16),
            pltpu.VMEM((slots, 2 * chunks, LANES), F32),
            pltpu.VMEM((beam_window.shape[0], shard), F32),
            pltpu.VMEM((chans, shard), F32),
            pltpu.VMEM((slots, 4 * blks * blks, LANES), BF16),
            pltpu.VMEM((slots, 4 * blks * blks, LANES), F32),
            pltpu.VMEM((chans, lanes), F32),
            pltpu.VMEM((chans, blks, chans, lanes), F32),
            pltpu.VMEM((blks, 2, lanes), F32),
            pltpu.VMEM((blks, 2 * chans, lanes), F32),
            pltpu.VMEM((chans, lanes), F32),
            pltpu.VMEM((2, lanes), F32),
            pltpu.VMEM((blks, lanes // LANES, 2 * chans, LANES), F32),
            pltpu.SemaphoreType.DMA((10,)),
            pltpu.SemaphoreType.DMA((2,)),
            pltpu.SemaphoreType.DMA((2,)),
        ],
        compiler_params=pltpu.CompilerParams(collective_id=0, has_side_effects=True),
        name="normal_product",
    )(
        comp_alms, jnp.swapaxes(legendre, 2, 3), noise, beam_window, mixing, channel_of,
        m_orders, cycle_of, cycle_pixels, cycle_of.reshape(1, cycles),
    )
    return result.reshape(comp_alms.shape)


def solution(mesh):
    in_specs = (
        P(None, None, "blk", "chan"),
        P(None, "blk", None, None),
        P("chan", None, "blk", None),
        P(),
        P(),
        P(),
        P(),
        P(),
        P(),
    )
    out_specs = P(None, None, "blk", "chan")
    work = functools.partial(body, mesh.shape["chan"], mesh.shape["blk"])
    return jax.shard_map(work, mesh=mesh, in_specs=in_specs, out_specs=out_specs, check_vma=False)
```

```python
import functools
import math

import jax
import jax.numpy as jnp
from jax import lax
from jax.experimental import pallas as pl
from jax.experimental.pallas import tpu as pltpu
from jax.sharding import PartitionSpec as P

F32 = jnp.float32
BF16 = jnp.bfloat16
LANES = 128
NT = (((1,), (1,)), ((), ()))
NN = (((1,), (0,)), ((), ()))


def iota(shape, dim):
    return lax.broadcasted_iota(jnp.int32, shape, dim)


def dot(left, right, dims):
    return lax.dot_general(left, right, dims, preferred_element_type=F32)


def rest(value, size):
    return value & (size - 1) if size & (size - 1) == 0 else lax.rem(value, jnp.int32(size))


def share(value, size):
    if size & (size - 1) == 0:
        return value >> (size.bit_length() - 1)
    return lax.div(value, jnp.int32(size))


def turn(steps, count, double_inverse):
    quarter = jnp.floor(steps * double_inverse + 0.5)
    angle = (2.0 * steps - quarter * count) * (double_inverse * jnp.float32(math.pi / 4))
    square = angle * angle
    sine = angle + angle * square * (
        (-1.9515295891e-4 * square + 8.3321608736e-3) * square - 1.6666654611e-1
    )
    cosine = (1.0 - 0.5 * square) + square * square * (
        (2.443315711809948e-5 * square - 1.388731625493765e-3) * square + 4.166664568298827e-2
    )
    index = quarter.astype(jnp.int32)
    odd = (index & 1) == 1
    real = jnp.where(odd, sine, cosine)
    imag = jnp.where(odd, cosine, sine)
    real = jnp.where(((index + 1) & 2) == 2, -real, real)
    imag = jnp.where((index & 2) == 2, -imag, imag)
    return real, imag


def pair_turns(cosines, sines, order):
    cos_one, sin_one = cosines[order : order + 1], sines[order : order + 1]
    cos_cos, sin_sin = cos_one * cosines, sin_one * sines
    sin_cos, cos_sin = sin_one * cosines, cos_one * sines
    return [cos_cos - sin_sin, sin_cos + cos_sin, cos_cos + sin_sin, sin_cos - cos_sin]


def kernel(
    chans, blks, alm_hbm, leg_hbm, inv_hbm, beam_hbm, mix_hbm, chan_hbm, order_hbm, cycle_hbm,
    pixel_hbm, cycle_row_hbm, out_ref, mix_s, chan_s, order_s, cycle_s, pixel_s, cycle_row, comp_v,
    leg_v, inv_v, beam_v, gain_v, fine_v, coarse_v, send1, recv1, send2, recv2, spare1, spare2, twin_v,
    in_sem, send_sem, recv_sem,
):
    comps = comp_v.shape[0]
    shard = comp_v.shape[2]
    cycles = leg_v.shape[1]
    slots = inv_v.shape[0]
    chunks = inv_v.shape[1] // 2
    rows = 4 * chans
    lanes = 4 * cycles
    total = chans * blks
    me_c = lax.axis_index("chan")
    me_b = lax.axis_index("blk")
    first = pl.multiple_of(me_c * shard, shard)

    me = me_b * chans + me_c

    def peer(offset):
        index = offset - 1 + (me < offset).astype(jnp.int32)
        return rest(index, chans), share(index, chans)

    def each(first_offset, last_offset, act):
        if last_offset - first_offset <= 64:
            for offset in range(first_offset, last_offset):
                act(offset)
        else:
            lax.fori_loop(
                first_offset, last_offset, lambda offset, carry: (act(offset), carry)[1], 0
            )

    barrier = pltpu.get_barrier_semaphore()

    def tell(semaphore, dest_c, dest_b):
        pl.semaphore_signal(
            semaphore,
            inc=1,
            device_id=(dest_c, dest_b),
            device_id_type=pl.DeviceIdType.MESH,
        )

    scalars = []

    def load(src, dst, group):
        copy = pltpu.make_async_copy(src, dst, in_sem.at[group])
        copy.start()
        return copy

    def loaded(dst, group):
        pltpu.make_async_copy(dst, dst, in_sem.at[group]).wait()

    for src, dst in (
        (order_hbm, order_s), (cycle_hbm, cycle_s), (pixel_hbm, pixel_s), (mix_hbm, mix_s),
        (chan_hbm, chan_s), (cycle_row_hbm, cycle_row),
    ):
        scalars.append(load(src, dst, 4 + len(scalars)))
    for kind in range(2):
        load(leg_hbm.at[kind, 0, :, pl.ds(first, shard)], leg_v.at[kind], 2)
    for comp in range(comps):
        for half in range(2):
            load(alm_hbm.at[comp, :, 0, :], comp_v.at[comp, pl.ds(4 * half, 4), :], 0)
    load(beam_hbm.at[:, pl.ds(first, shard)], beam_v, 1)
    for stokes in range(2):
        for slot in range(slots):
            load(
                inv_hbm.at[stokes, :, slot, :],
                inv_v.at[slot, pl.ds(stokes * chunks, chunks), :],
                3,
            )
    each(
        1,
        total,
        lambda offset: tell(
            barrier, rest(me_c + offset // blks, chans), rest(me_b + offset % blks, blks)
        ),
    )
    for copy in scalars:
        copy.wait()

    own_cycles = [cycle_s[me_b * slots + slot] for slot in range(slots)]
    own_pixels = [pixel_s[cycle].astype(F32) for cycle in own_cycles]

    def by_slot(slot_index, values):
        result = jnp.where(slot_index == 0, values[0], values[slots - 1])
        for slot in range(1, slots - 1):
            result = jnp.where(slot_index == slot, values[slot], result)
        return result

    grid = (blks, LANES)
    row = iota(grid, 0)
    lane = iota(grid, 1)
    orders = jnp.full(grid, order_s[0], jnp.int32)
    for order in range(1, blks):
        orders = jnp.where(row == order, order_s[order], orders)
    orders = orders.astype(F32)
    fine = orders * (2 * lane + 1).astype(F32)
    leap = orders * (2.0 * LANES)
    chunk = rest(lane, chunks).astype(F32)
    def table(slot):
        pixels = jnp.full(grid, own_pixels[slot], F32)
        reciprocal = 1.0 / pixels
        stride = leap - jnp.floor(leap * (0.5 * reciprocal)) * (2.0 * pixels)
        fine_turn = turn(fine, pixels, 2.0 * reciprocal)
        short = pixels <= float(LANES)
        fine_turn = [
            jnp.where(short, value.astype(BF16).astype(F32), value) for value in fine_turn
        ]
        coarse_turn = turn(stride * chunk, pixels, 2.0 * reciprocal)
        for order in range(blks):
            block = pl.ds(order * 4 * blks, 4 * blks)
            fine_v[slot, block, :] = jnp.concatenate(
                pair_turns(*fine_turn, order), axis=0
            ).astype(BF16)
            coarse_v[slot, block, :] = jnp.concatenate(pair_turns(*coarse_turn, order), axis=0)

    for slot in range(3):
        table(slot)
    loaded(comp_v, 0)
    loaded(beam_v, 1)
    loaded(leg_v, 2)
    for slot in range(3, slots):
        table(slot)

    low_half = iota((8, 1), 0) < 4
    keep = (iota((1, shard), 1) + first >= order_s[me_b]).astype(F32)
    alm_rows = []
    for pair in range(chans // 2):
        picked = [chan_s[2 * pair], chan_s[2 * pair + 1]]
        columns = [
            jnp.where(low_half, mix_s[picked[0], comp], mix_s[picked[1], comp])
            for comp in range(comps)
        ]
        mixed = columns[0] * comp_v[0]
        for comp in range(1, comps):
            mixed = mixed + columns[comp] * comp_v[comp]
        gains = [beam_v[pl.ds(chan, 1), :] * keep for chan in picked]
        gain_v[pl.ds(2 * pair, 1), :] = gains[0]
        gain_v[pl.ds(2 * pair + 1, 1), :] = gains[1]
        alm_rows.append(mixed * jnp.where(low_half, gains[0], gains[1]))
    alm = jnp.concatenate(alm_rows, axis=0).astype(BF16)
    plus = dot(alm, jnp.concatenate([leg_v[0]] * 4, axis=0), NT)
    minus = dot(alm, jnp.concatenate([leg_v[1]] * 4, axis=0), NT)
    row_part = iota(plus.shape, 0) % 4
    lane_part = iota(plus.shape, 1) // cycles
    outer = (lane_part == 0) | (lane_part == 3)
    signed = jnp.where(outer, -minus, minus)
    joined = jnp.where(lane_part == row_part, plus, 0.0) + jnp.where(
        lane_part == 3 - row_part, signed, 0.0
    )
    folded = joined
    for step in range(1, 4):
        folded = folded + pltpu.roll(joined, rows - step, 0)
    for chan in range(chans):
        send1[pl.ds(chan, 1), :] = folded[4 * chan : 4 * chan + 1]


    def arrived(dst, phase):
        pltpu.make_async_copy(dst, dst, recv_sem.at[phase]).wait()

    def sent(dst, phase):
        pltpu.make_async_copy(dst, dst, send_sem.at[phase]).wait()

    def routes(dest_b):
        return (
            (send1, recv1.at[me_c, me_b]),
            (send2.at[dest_b], recv2.at[me_b, pl.ds(2 * me_c, 2), :]),
        )

    def post(offset, phase):
        dest_c, dest_b = peer(offset)
        src, dst = routes(dest_b)[phase]
        pltpu.make_async_remote_copy(
            src_ref=src,
            dst_ref=dst,
            send_sem=send_sem.at[phase],
            recv_sem=recv_sem.at[phase],
            device_id=(dest_c, dest_b),
            device_id_type=pl.DeviceIdType.MESH,
        ).start()

    early = min(4, total - 1)
    pl.semaphore_wait(barrier, total - 1)
    each(1, early + 1, lambda offset: post(offset, 0))
    loaded(inv_v, 3)
    grid = (2 * chunks, LANES)
    pixel_index = rest(iota(grid, 0), chunks) * LANES + iota(grid, 1)
    parts = [[] for _ in range(blks)]
    for slot in range(slots):
        live = pixel_index.astype(F32) < own_pixels[slot]
        noise = jnp.where(live, inv_v[slot], 0.0).astype(BF16)
        inner = dot(fine_v[slot], noise, NT)
        for order in range(blks):
            base = order * 4 * blks
            held = [inner[base + kind * blks : base + (kind + 1) * blks] for kind in range(4)]
            outer_turn = [
                coarse_v[slot, pl.ds(base + kind * blks, blks), :] for kind in range(4)
            ]
            add_real = outer_turn[0] * held[0] - outer_turn[1] * held[1]
            add_imag = outer_turn[0] * held[1] + outer_turn[1] * held[0]
            sub_real = outer_turn[2] * held[2] - outer_turn[3] * held[3]
            sub_imag = outer_turn[2] * held[3] + outer_turn[3] * held[2]
            blocks = jnp.concatenate(
                [
                    sub_real + add_real,
                    sub_imag - add_imag,
                    -sub_imag - add_imag,
                    sub_real - add_real,
                ],
                axis=0,
            )
            high = blocks.astype(BF16)
            parts[order].append((high, (blocks - high.astype(F32)).astype(BF16)))
    ones = (
        share(rest(iota((8, 2 * LANES), 1), LANES), chunks) == iota((8, 2 * LANES), 0)
    ).astype(F32).astype(BF16)
    weight = 0.5 / by_slot(share(iota((2, lanes), 1), 4 * blks), own_pixels)
    for order in range(blks):
        halves = [jnp.concatenate(pair, axis=1) for pair in parts[order]]
        summed = dot(ones, jnp.concatenate(halves, axis=0), NT)
        send2[order] = summed[0:2] * weight
    each(1, early + 1, lambda offset: post(offset, 1))
    each(early + 1, total, lambda offset: (post(offset, 0), post(offset, 1)))
    for phase, (src, dst) in enumerate(routes(me_b)):
        pltpu.make_async_copy(src, dst, recv_sem.at[phase]).start()
        pltpu.make_async_copy(src, (spare1, spare2)[phase], send_sem.at[phase]).start()

    to_lane = iota((cycles, lanes), 1)
    spread = (
        iota((cycles, lanes), 0) == rest(to_lane, blks) * slots + share(to_lane, 4 * blks)
    ).astype(F32).astype(BF16)
    lane_cycle = dot(
        jnp.broadcast_to(cycle_row[...].astype(F32), (8, cycles)).astype(BF16), spread, NN
    )[0:1]
    half = (2 * cycles, lanes)
    from_row = iota(half, 0)
    shuffle = (
        (rest(from_row, cycles).astype(F32) == lane_cycle)
        & (share(from_row, cycles) == (share(iota(half, 1), blks) & 1))
    ).astype(F32)
    leg_stack = jnp.concatenate([leg_v[0], leg_v[1]], axis=0)
    back_leg = dot(shuffle.T.astype(BF16), leg_stack, NN).astype(BF16)
    empty = jnp.zeros(half, F32)
    shuffle = jnp.concatenate(
        [
            jnp.concatenate([shuffle, empty], axis=1),
            jnp.concatenate([empty, shuffle], axis=1),
        ],
        axis=0,
    ).astype(BF16)

    arrived(recv1, 0)
    gathered = []
    for order in range(blks):
        coeffs = recv1[0, order]
        for chan in range(1, chans):
            coeffs = coeffs + recv1[chan, order]
        gathered.append(coeffs)
    coeffs = dot(jnp.concatenate(gathered, axis=0).astype(BF16), shuffle, NN)
    for order in range(blks):
        own = coeffs[order * chans : (order + 1) * chans]
        for tile in range(lanes // LANES):
            for part in range(2):
                begin = part * lanes + tile * LANES
                twin_v[order, tile, pl.ds(part, chans, stride=2), :] = own[
                    :, begin : begin + LANES
                ]
    turned = [
        jnp.concatenate([twin_v[order, tile] for tile in range(lanes // LANES)], axis=1)
        for order in range(blks)
    ]
    low_lane = iota((2 * chans, lanes), 1)
    step = 1
    while step < blks:
        upper = (share(low_lane, step) & 1) == 1
        following = list(turned)
        for order in range(blks):
            if (order // step) % 2 == 0:
                one, two = turned[order], turned[order + step]
                following[order] = jnp.where(upper, pltpu.roll(two, step, 1), one)
                following[order + step] = jnp.where(
                    upper, two, pltpu.roll(one, lanes - step, 1)
                )
        turned = following
        step *= 2

    final_row = iota((8, lanes), 0)
    final_lane = iota((8, lanes), 1)
    row_real = final_row & 1
    row_stokes = (final_row >> 1) & 1
    lane_kind = share(final_lane, blks) & 1
    lane_real = share(final_lane, 2 * blks) & 1
    straight = (lane_kind == 0) & (lane_real == row_real)
    crossed = (lane_kind == 1) & (lane_real != row_real)
    cross_sign = jnp.where(row_stokes == row_real, -1.0, 1.0)
    mask = [
        jnp.where(straight & (row_stokes == stokes), 1.0, 0.0)
        + jnp.where(crossed & (row_stokes != stokes), cross_sign, 0.0)
        for stokes in range(2)
    ]

    arrived(recv2, 1)
    sums = [recv2[block] * turned[block] for block in range(blks)]
    step = blks // 2
    while step >= 1:
        upper = (share(low_lane, step) & 1) == 1
        merged = []
        for block in range(step):
            one, two = sums[block], sums[block + step]
            kept = jnp.where(upper, two, one)
            moved = jnp.where(upper, one, two)
            merged.append(
                kept
                + jnp.where(
                    upper, pltpu.roll(moved, step, 1), pltpu.roll(moved, lanes - step, 1)
                )
            )
        sums = merged
        step //= 2
    total_sum = sums[0]
    odd_part = (share(iota(total_sum.shape, 1), blks) & 1) == 1
    total_sum = total_sum + jnp.where(
        odd_part, pltpu.roll(total_sum, blks, 1), pltpu.roll(total_sum, lanes - blks, 1)
    )
    total_sum = total_sum.astype(BF16).astype(F32)
    left = jnp.concatenate(
        [
            mask[0] * total_sum[2 * chan : 2 * chan + 1]
            + mask[1] * total_sum[2 * chan + 1 : 2 * chan + 2]
            for chan in range(chans)
        ],
        axis=0,
    )
    alm_grads = dot(left.astype(BF16), back_leg, NN)
    scaled = [
        alm_grads[8 * chan : 8 * chan + 8] * gain_v[pl.ds(chan, 1), :] for chan in range(chans)
    ]
    for comp in range(comps):
        mixed = mix_s[chan_s[0], comp] * scaled[0]
        for chan in range(1, chans):
            mixed = mixed + mix_s[chan_s[chan], comp] * scaled[chan]
        out_ref[comp] = mixed[0:4]
    sent(recv1, 0)
    sent(recv2, 1)


def body(
    chans, blks, comp_alms, legendre, inv_noise, beam_window, mixing, channel_of, m_orders,
    cycle_of, cycle_pixels,
):
    comps, parts, order_dev, shard = comp_alms.shape
    cycles = legendre.shape[3]
    chan_dev, stokes, slots, width = inv_noise.shape
    assert parts == 4 and stokes == 2 and order_dev == 1 and chan_dev == 1
    lanes = 4 * cycles
    assert slots * blks == cycles
    chunks = width // LANES
    assert 2 * chunks == LANES
    noise = jnp.swapaxes(inv_noise.reshape(stokes, slots, chunks, LANES), 1, 2)
    any_space = pl.BlockSpec(memory_space=pl.ANY)
    vector = pl.BlockSpec(memory_space=pltpu.VMEM)
    result = pl.pallas_call(
        functools.partial(kernel, chans, blks),
        out_shape=pltpu.VMEM((comps, 4, shard), F32),
        in_specs=[any_space] * 10,
        out_specs=vector,
        scratch_shapes=[
            pltpu.SMEM(mixing.shape, F32),
            pltpu.SMEM(channel_of.shape, jnp.int32),
            pltpu.SMEM(m_orders.shape, jnp.int32),
            pltpu.SMEM(cycle_of.shape, jnp.int32),
            pltpu.SMEM(cycle_pixels.shape, jnp.int32),
            pltpu.VMEM((1, cycles), jnp.int32),
            pltpu.VMEM((comps, 8, shard), F32),
            pltpu.VMEM((2, cycles, shard), BF16),
            pltpu.VMEM((slots, 2 * chunks, LANES), F32),
            pltpu.VMEM((beam_window.shape[0], shard), F32),
            pltpu.VMEM((chans, shard), F32),
            pltpu.VMEM((slots, 4 * blks * blks, LANES), BF16),
            pltpu.VMEM((slots, 4 * blks * blks, LANES), F32),
            pltpu.VMEM((chans, lanes), F32),
            pltpu.VMEM((chans, blks, chans, lanes), F32),
            pltpu.VMEM((blks, 2, lanes), F32),
            pltpu.VMEM((blks, 2 * chans, lanes), F32),
            pltpu.VMEM((chans, lanes), F32),
            pltpu.VMEM((2, lanes), F32),
            pltpu.VMEM((blks, lanes // LANES, 2 * chans, LANES), F32),
            pltpu.SemaphoreType.DMA((10,)),
            pltpu.SemaphoreType.DMA((2,)),
            pltpu.SemaphoreType.DMA((2,)),
        ],
        compiler_params=pltpu.CompilerParams(collective_id=0, has_side_effects=True),
        name="normal_product",
    )(
        comp_alms, jnp.swapaxes(legendre, 2, 3), noise, beam_window, mixing, channel_of,
        m_orders, cycle_of, cycle_pixels, cycle_of.reshape(1, cycles),
    )
    return result.reshape(comp_alms.shape)


def solution(mesh):
    in_specs = (
        P(None, None, "blk", "chan"),
        P(None, "blk", None, None),
        P("chan", None, "blk", None),
        P(),
        P(),
        P(),
        P(),
        P(),
        P(),
    )
    out_specs = P(None, None, "blk", "chan")
    work = functools.partial(body, mesh.shape["chan"], mesh.shape["blk"])
    return jax.shard_map(work, mesh=mesh, in_specs=in_specs, out_specs=out_specs, check_vma=False)
```

```python
import functools
import math

import jax
import jax.numpy as jnp
from jax import lax
from jax.experimental import pallas as pl
from jax.experimental.pallas import tpu as pltpu
from jax.sharding import PartitionSpec as P

F32 = jnp.float32
BF16 = jnp.bfloat16
LANES = 128
NT = (((1,), (1,)), ((), ()))
NN = (((1,), (0,)), ((), ()))


def iota(shape, dim):
    return lax.broadcasted_iota(jnp.int32, shape, dim)


def dot(left, right, dims):
    return lax.dot_general(left, right, dims, preferred_element_type=F32)


def rest(value, size):
    return value & (size - 1) if size & (size - 1) == 0 else lax.rem(value, jnp.int32(size))


def share(value, size):
    if size & (size - 1) == 0:
        return value >> (size.bit_length() - 1)
    return lax.div(value, jnp.int32(size))


def turn(steps, count, double_inverse):
    quarter = jnp.floor(steps * double_inverse + 0.5)
    angle = (2.0 * steps - quarter * count) * (double_inverse * jnp.float32(math.pi / 4))
    square = angle * angle
    sine = angle + angle * square * (
        (-1.9515295891e-4 * square + 8.3321608736e-3) * square - 1.6666654611e-1
    )
    cosine = (1.0 - 0.5 * square) + square * square * (
        (2.443315711809948e-5 * square - 1.388731625493765e-3) * square + 4.166664568298827e-2
    )
    index = quarter.astype(jnp.int32)
    odd = (index & 1) == 1
    real = jnp.where(odd, sine, cosine)
    imag = jnp.where(odd, cosine, sine)
    real = jnp.where(((index + 1) & 2) == 2, -real, real)
    imag = jnp.where((index & 2) == 2, -imag, imag)
    return real, imag


def pair_turns(cosines, sines, order):
    cos_one, sin_one = cosines[order : order + 1], sines[order : order + 1]
    cos_cos, sin_sin = cos_one * cosines, sin_one * sines
    sin_cos, cos_sin = sin_one * cosines, cos_one * sines
    return [cos_cos - sin_sin, sin_cos + cos_sin, cos_cos + sin_sin, sin_cos - cos_sin]


def kernel(
    chans, blks, alm_hbm, leg_hbm, inv_hbm, beam_hbm, mix_hbm, chan_hbm, order_hbm, cycle_hbm,
    pixel_hbm, cycle_row_hbm, out_ref, mix_s, chan_s, order_s, cycle_s, pixel_s, cycle_row, comp_v,
    leg_v, inv_v, beam_v, gain_v, fine_v, coarse_v, send1, recv1, send2, recv2, spare1, spare2, twin_v,
    in_sem, send_sem, recv_sem,
):
    comps = comp_v.shape[0]
    shard = comp_v.shape[2]
    cycles = leg_v.shape[1]
    slots = inv_v.shape[0]
    chunks = inv_v.shape[1] // 2
    rows = 4 * chans
    lanes = 4 * cycles
    total = chans * blks
    me_c = lax.axis_index("chan")
    me_b = lax.axis_index("blk")
    first = pl.multiple_of(me_c * shard, shard)

    me = me_b * chans + me_c

    def peer(offset):
        index = offset - 1 + (me < offset).astype(jnp.int32)
        return rest(index, chans), share(index, chans)

    def each(first_offset, last_offset, act):
        if last_offset - first_offset <= 64:
            for offset in range(first_offset, last_offset):
                act(offset)
        else:
            lax.fori_loop(
                first_offset, last_offset, lambda offset, carry: (act(offset), carry)[1], 0
            )

    barrier = pltpu.get_barrier_semaphore()

    def tell(semaphore, dest_c, dest_b):
        pl.semaphore_signal(
            semaphore,
            inc=1,
            device_id=(dest_c, dest_b),
            device_id_type=pl.DeviceIdType.MESH,
        )

    scalars = []

    def load(src, dst, group):
        copy = pltpu.make_async_copy(src, dst, in_sem.at[group])
        copy.start()
        return copy

    def loaded(dst, group):
        pltpu.make_async_copy(dst, dst, in_sem.at[group]).wait()

    for src, dst in (
        (order_hbm, order_s), (cycle_hbm, cycle_s), (pixel_hbm, pixel_s), (mix_hbm, mix_s),
        (chan_hbm, chan_s), (cycle_row_hbm, cycle_row),
    ):
        scalars.append(load(src, dst, 4 + len(scalars)))
    for kind in range(2):
        load(leg_hbm.at[kind, 0, :, pl.ds(first, shard)], leg_v.at[kind], 2)
    for comp in range(comps):
        for half in range(2):
            load(alm_hbm.at[comp, :, 0, :], comp_v.at[comp, pl.ds(4 * half, 4), :], 0)
    load(beam_hbm.at[:, pl.ds(first, shard)], beam_v, 1)
    for stokes in range(2):
        for slot in range(slots):
            load(
                inv_hbm.at[stokes, :, slot, :],
                inv_v.at[slot, pl.ds(stokes * chunks, chunks), :],
                3,
            )
    each(
        1,
        total,
        lambda offset: tell(
            barrier, rest(me_c + offset // blks, chans), rest(me_b + offset % blks, blks)
        ),
    )
    for copy in scalars:
        copy.wait()

    own_cycles = [cycle_s[me_b * slots + slot] for slot in range(slots)]
    own_pixels = [pixel_s[cycle].astype(F32) for cycle in own_cycles]

    def by_slot(slot_index, values):
        result = jnp.where(slot_index == 0, values[0], values[slots - 1])
        for slot in range(1, slots - 1):
            result = jnp.where(slot_index == slot, values[slot], result)
        return result

    grid = (blks, LANES)
    row = iota(grid, 0)
    lane = iota(grid, 1)
    orders = jnp.full(grid, order_s[0], jnp.int32)
    for order in range(1, blks):
        orders = jnp.where(row == order, order_s[order], orders)
    orders = orders.astype(F32)
    fine = orders * (2 * lane + 1).astype(F32)
    leap = orders * (2.0 * LANES)
    chunk = rest(lane, chunks).astype(F32)
    def table(slot):
        pixels = jnp.full(grid, own_pixels[slot], F32)
        reciprocal = 1.0 / pixels
        stride = leap - jnp.floor(leap * (0.5 * reciprocal)) * (2.0 * pixels)
        fine_turn = turn(fine, pixels, 2.0 * reciprocal)
        short = pixels <= float(LANES)
        fine_turn = [
            jnp.where(short, value.astype(BF16).astype(F32), value) for value in fine_turn
        ]
        coarse_turn = turn(stride * chunk, pixels, 2.0 * reciprocal)
        for order in range(blks):
            block = pl.ds(order * 4 * blks, 4 * blks)
            fine_v[slot, block, :] = jnp.concatenate(
                pair_turns(*fine_turn, order), axis=0
            ).astype(BF16)
            coarse_v[slot, block, :] = jnp.concatenate(pair_turns(*coarse_turn, order), axis=0)

    for slot in range(slots):
        table(slot)
    loaded(comp_v, 0)
    loaded(beam_v, 1)
    loaded(leg_v, 2)
    low_half = iota((8, 1), 0) < 4
    keep = (iota((1, shard), 1) + first >= order_s[me_b]).astype(F32)
    alm_rows = []
    for pair in range(chans // 2):
        picked = [chan_s[2 * pair], chan_s[2 * pair + 1]]
        columns = [
            jnp.where(low_half, mix_s[picked[0], comp], mix_s[picked[1], comp])
            for comp in range(comps)
        ]
        mixed = columns[0] * comp_v[0]
        for comp in range(1, comps):
            mixed = mixed + columns[comp] * comp_v[comp]
        gains = [beam_v[pl.ds(chan, 1), :] * keep for chan in picked]
        gain_v[pl.ds(2 * pair, 1), :] = gains[0]
        gain_v[pl.ds(2 * pair + 1, 1), :] = gains[1]
        alm_rows.append(mixed * jnp.where(low_half, gains[0], gains[1]))
    alm = jnp.concatenate(alm_rows, axis=0).astype(BF16)
    plus = dot(alm, jnp.concatenate([leg_v[0]] * 4, axis=0), NT)
    minus = dot(alm, jnp.concatenate([leg_v[1]] * 4, axis=0), NT)
    row_part = iota(plus.shape, 0) % 4
    lane_part = iota(plus.shape, 1) // cycles
    outer = (lane_part == 0) | (lane_part == 3)
    signed = jnp.where(outer, -minus, minus)
    joined = jnp.where(lane_part == row_part, plus, 0.0) + jnp.where(
        lane_part == 3 - row_part, signed, 0.0
    )
    folded = joined
    for step in range(1, 4):
        folded = folded + pltpu.roll(joined, rows - step, 0)
    for chan in range(chans):
        send1[pl.ds(chan, 1), :] = folded[4 * chan : 4 * chan + 1]


    def arrived(dst, phase):
        pltpu.make_async_copy(dst, dst, recv_sem.at[phase]).wait()

    def sent(dst, phase):
        pltpu.make_async_copy(dst, dst, send_sem.at[phase]).wait()

    def routes(dest_b):
        return (
            (send1, recv1.at[me_c, me_b]),
            (send2.at[dest_b], recv2.at[me_b, pl.ds(2 * me_c, 2), :]),
        )

    def post(offset, phase):
        dest_c, dest_b = peer(offset)
        src, dst = routes(dest_b)[phase]
        pltpu.make_async_remote_copy(
            src_ref=src,
            dst_ref=dst,
            send_sem=send_sem.at[phase],
            recv_sem=recv_sem.at[phase],
            device_id=(dest_c, dest_b),
            device_id_type=pl.DeviceIdType.MESH,
        ).start()

    early = min(4, total - 1)
    pl.semaphore_wait(barrier, total - 1)
    each(1, early + 1, lambda offset: post(offset, 0))
    loaded(inv_v, 3)
    grid = (2 * chunks, LANES)
    pixel_index = rest(iota(grid, 0), chunks) * LANES + iota(grid, 1)
    parts = [[] for _ in range(blks)]
    for slot in range(slots):
        live = pixel_index.astype(F32) < own_pixels[slot]
        noise = jnp.where(live, inv_v[slot], 0.0).astype(BF16)
        inner = dot(fine_v[slot], noise, NT)
        for order in range(blks):
            base = order * 4 * blks
            held = [inner[base + kind * blks : base + (kind + 1) * blks] for kind in range(4)]
            outer_turn = [
                coarse_v[slot, pl.ds(base + kind * blks, blks), :] for kind in range(4)
            ]
            add_real = outer_turn[0] * held[0] - outer_turn[1] * held[1]
            add_imag = outer_turn[0] * held[1] + outer_turn[1] * held[0]
            sub_real = outer_turn[2] * held[2] - outer_turn[3] * held[3]
            sub_imag = outer_turn[2] * held[3] + outer_turn[3] * held[2]
            blocks = jnp.concatenate(
                [
                    sub_real + add_real,
                    sub_imag - add_imag,
                    -sub_imag - add_imag,
                    sub_real - add_real,
                ],
                axis=0,
            )
            high = blocks.astype(BF16)
            parts[order].append((high, (blocks - high.astype(F32)).astype(BF16)))
    ones = (
        share(rest(iota((8, 2 * LANES), 1), LANES), chunks) == iota((8, 2 * LANES), 0)
    ).astype(F32).astype(BF16)
    weight = 0.5 / by_slot(share(iota((2, lanes), 1), 4 * blks), own_pixels)
    for order in range(blks):
        halves = [jnp.concatenate(pair, axis=1) for pair in parts[order]]
        summed = dot(ones, jnp.concatenate(halves, axis=0), NT)
        send2[order] = summed[0:2] * weight
    each(1, early + 1, lambda offset: post(offset, 1))
    each(early + 1, total, lambda offset: (post(offset, 0), post(offset, 1)))
    for phase, (src, dst) in enumerate(routes(me_b)):
        pltpu.make_async_copy(src, dst, recv_sem.at[phase]).start()
        pltpu.make_async_copy(src, (spare1, spare2)[phase], send_sem.at[phase]).start()

    to_lane = iota((cycles, lanes), 1)
    spread = (
        iota((cycles, lanes), 0) == rest(to_lane, blks) * slots + share(to_lane, 4 * blks)
    ).astype(F32).astype(BF16)
    lane_cycle = dot(
        jnp.broadcast_to(cycle_row[...].astype(F32), (8, cycles)).astype(BF16), spread, NN
    )[0:1]
    half = (2 * cycles, lanes)
    from_row = iota(half, 0)
    shuffle = (
        (rest(from_row, cycles).astype(F32) == lane_cycle)
        & (share(from_row, cycles) == (share(iota(half, 1), blks) & 1))
    ).astype(F32)
    leg_stack = jnp.concatenate([leg_v[0], leg_v[1]], axis=0)
    back_leg = dot(shuffle.T.astype(BF16), leg_stack, NN).astype(BF16)
    empty = jnp.zeros(half, F32)
    shuffle = jnp.concatenate(
        [
            jnp.concatenate([shuffle, empty], axis=1),
            jnp.concatenate([empty, shuffle], axis=1),
        ],
        axis=0,
    ).astype(BF16)

    arrived(recv1, 0)
    gathered = []
    for order in range(blks):
        coeffs = recv1[0, order]
        for chan in range(1, chans):
            coeffs = coeffs + recv1[chan, order]
        gathered.append(coeffs)
    coeffs = dot(jnp.concatenate(gathered, axis=0).astype(BF16), shuffle, NN)
    for order in range(blks):
        own = coeffs[order * chans : (order + 1) * chans]
        for tile in range(lanes // LANES):
            for part in range(2):
                begin = part * lanes + tile * LANES
                twin_v[order, tile, pl.ds(part, chans, stride=2), :] = own[
                    :, begin : begin + LANES
                ]
    turned = [
        jnp.concatenate([twin_v[order, tile] for tile in range(lanes // LANES)], axis=1)
        for order in range(blks)
    ]
    low_lane = iota((2 * chans, lanes), 1)
    step = 1
    while step < blks:
        upper = (share(low_lane, step) & 1) == 1
        following = list(turned)
        for order in range(blks):
            if (order // step) % 2 == 0:
                one, two = turned[order], turned[order + step]
                following[order] = jnp.where(upper, pltpu.roll(two, step, 1), one)
                following[order + step] = jnp.where(
                    upper, two, pltpu.roll(one, lanes - step, 1)
                )
        turned = following
        step *= 2

    final_row = iota((8, lanes), 0)
    final_lane = iota((8, lanes), 1)
    row_real = final_row & 1
    row_stokes = (final_row >> 1) & 1
    lane_kind = share(final_lane, blks) & 1
    lane_real = share(final_lane, 2 * blks) & 1
    straight = (lane_kind == 0) & (lane_real == row_real)
    crossed = (lane_kind == 1) & (lane_real != row_real)
    cross_sign = jnp.where(row_stokes == row_real, -1.0, 1.0)
    mask = [
        jnp.where(straight & (row_stokes == stokes), 1.0, 0.0)
        + jnp.where(crossed & (row_stokes != stokes), cross_sign, 0.0)
        for stokes in range(2)
    ]

    arrived(recv2, 1)
    sums = [recv2[block] * turned[block] for block in range(blks)]
    step = blks // 2
    while step >= 1:
        upper = (share(low_lane, step) & 1) == 1
        merged = []
        for block in range(step):
            one, two = sums[block], sums[block + step]
            kept = jnp.where(upper, two, one)
            moved = jnp.where(upper, one, two)
            merged.append(
                kept
                + jnp.where(
                    upper, pltpu.roll(moved, step, 1), pltpu.roll(moved, lanes - step, 1)
                )
            )
        sums = merged
        step //= 2
    total_sum = sums[0]
    odd_part = (share(iota(total_sum.shape, 1), blks) & 1) == 1
    total_sum = total_sum + jnp.where(
        odd_part, pltpu.roll(total_sum, blks, 1), pltpu.roll(total_sum, lanes - blks, 1)
    )
    total_sum = total_sum.astype(BF16).astype(F32)
    left = jnp.concatenate(
        [
            mask[0] * total_sum[2 * chan : 2 * chan + 1]
            + mask[1] * total_sum[2 * chan + 1 : 2 * chan + 2]
            for chan in range(chans)
        ],
        axis=0,
    )
    alm_grads = dot(left.astype(BF16), back_leg, NN)
    scaled = [
        alm_grads[8 * chan : 8 * chan + 8] * gain_v[pl.ds(chan, 1), :] for chan in range(chans)
    ]
    for comp in range(comps):
        mixed = mix_s[chan_s[0], comp] * scaled[0]
        for chan in range(1, chans):
            mixed = mixed + mix_s[chan_s[chan], comp] * scaled[chan]
        out_ref[comp] = mixed[0:4]
    sent(recv1, 0)
    sent(recv2, 1)


def body(
    chans, blks, comp_alms, legendre, inv_noise, beam_window, mixing, channel_of, m_orders,
    cycle_of, cycle_pixels,
):
    comps, parts, order_dev, shard = comp_alms.shape
    cycles = legendre.shape[3]
    chan_dev, stokes, slots, width = inv_noise.shape
    assert parts == 4 and stokes == 2 and order_dev == 1 and chan_dev == 1
    lanes = 4 * cycles
    assert slots * blks == cycles
    chunks = width // LANES
    assert 2 * chunks == LANES
    noise = jnp.swapaxes(inv_noise.reshape(stokes, slots, chunks, LANES), 1, 2)
    any_space = pl.BlockSpec(memory_space=pl.ANY)
    vector = pl.BlockSpec(memory_space=pltpu.VMEM)
    result = pl.pallas_call(
        functools.partial(kernel, chans, blks),
        out_shape=pltpu.VMEM((comps, 4, shard), F32),
        in_specs=[any_space] * 10,
        out_specs=vector,
        scratch_shapes=[
            pltpu.SMEM(mixing.shape, F32),
            pltpu.SMEM(channel_of.shape, jnp.int32),
            pltpu.SMEM(m_orders.shape, jnp.int32),
            pltpu.SMEM(cycle_of.shape, jnp.int32),
            pltpu.SMEM(cycle_pixels.shape, jnp.int32),
            pltpu.VMEM((1, cycles), jnp.int32),
            pltpu.VMEM((comps, 8, shard), F32),
            pltpu.VMEM((2, cycles, shard), BF16),
            pltpu.VMEM((slots, 2 * chunks, LANES), F32),
            pltpu.VMEM((beam_window.shape[0], shard), F32),
            pltpu.VMEM((chans, shard), F32),
            pltpu.VMEM((slots, 4 * blks * blks, LANES), BF16),
            pltpu.VMEM((slots, 4 * blks * blks, LANES), F32),
            pltpu.VMEM((chans, lanes), F32),
            pltpu.VMEM((chans, blks, chans, lanes), F32),
            pltpu.VMEM((blks, 2, lanes), F32),
            pltpu.VMEM((blks, 2 * chans, lanes), F32),
            pltpu.VMEM((chans, lanes), F32),
            pltpu.VMEM((2, lanes), F32),
            pltpu.VMEM((blks, lanes // LANES, 2 * chans, LANES), F32),
            pltpu.SemaphoreType.DMA((10,)),
            pltpu.SemaphoreType.DMA((2,)),
            pltpu.SemaphoreType.DMA((2,)),
        ],
        compiler_params=pltpu.CompilerParams(collective_id=0, has_side_effects=True),
        name="normal_product",
    )(
        comp_alms, jnp.swapaxes(legendre, 2, 3), noise, beam_window, mixing, channel_of,
        m_orders, cycle_of, cycle_pixels, cycle_of.reshape(1, cycles),
    )
    return result.reshape(comp_alms.shape)


def solution(mesh):
    in_specs = (
        P(None, None, "blk", "chan"),
        P(None, "blk", None, None),
        P("chan", None, "blk", None),
        P(),
        P(),
        P(),
        P(),
        P(),
        P(),
    )
    out_specs = P(None, None, "blk", "chan")
    work = functools.partial(body, mesh.shape["chan"], mesh.shape["blk"])
    return jax.shard_map(work, mesh=mesh, in_specs=in_specs, out_specs=out_specs, check_vma=False)
```

```python
import functools
import math

import jax
import jax.numpy as jnp
from jax import lax
from jax.experimental import pallas as pl
from jax.experimental.pallas import tpu as pltpu
from jax.sharding import PartitionSpec as P

F32 = jnp.float32
BF16 = jnp.bfloat16
LANES = 128
NT = (((1,), (1,)), ((), ()))
NN = (((1,), (0,)), ((), ()))


def iota(shape, dim):
    return lax.broadcasted_iota(jnp.int32, shape, dim)


def dot(left, right, dims):
    return lax.dot_general(left, right, dims, preferred_element_type=F32)


def rest(value, size):
    return value & (size - 1) if size & (size - 1) == 0 else lax.rem(value, jnp.int32(size))


def share(value, size):
    if size & (size - 1) == 0:
        return value >> (size.bit_length() - 1)
    return lax.div(value, jnp.int32(size))


def turn(steps, count, double_inverse):
    quarter = jnp.floor(steps * double_inverse + 0.5)
    angle = (2.0 * steps - quarter * count) * (double_inverse * jnp.float32(math.pi / 4))
    square = angle * angle
    sine = angle + angle * square * (
        (-1.9515295891e-4 * square + 8.3321608736e-3) * square - 1.6666654611e-1
    )
    cosine = (1.0 - 0.5 * square) + square * square * (
        (2.443315711809948e-5 * square - 1.388731625493765e-3) * square + 4.166664568298827e-2
    )
    index = quarter.astype(jnp.int32)
    odd = (index & 1) == 1
    real = jnp.where(odd, sine, cosine)
    imag = jnp.where(odd, cosine, sine)
    real = jnp.where(((index + 1) & 2) == 2, -real, real)
    imag = jnp.where((index & 2) == 2, -imag, imag)
    return real, imag


def pair_turns(cosines, sines, order):
    cos_one, sin_one = cosines[order : order + 1], sines[order : order + 1]
    cos_cos, sin_sin = cos_one * cosines, sin_one * sines
    sin_cos, cos_sin = sin_one * cosines, cos_one * sines
    return [cos_cos - sin_sin, sin_cos + cos_sin, cos_cos + sin_sin, sin_cos - cos_sin]


def kernel(
    chans, blks, alm_hbm, leg_hbm, inv_hbm, beam_hbm, mix_hbm, chan_hbm, order_hbm, cycle_hbm,
    pixel_hbm, cycle_row_hbm, out_ref, mix_s, chan_s, order_s, cycle_s, pixel_s, cycle_row, comp_v,
    leg_v, inv_v, beam_v, gain_v, fine_v, coarse_v, send1, recv1, send2, recv2, spare1, spare2, twin_v,
    in_sem, send_sem, recv_sem,
):
    comps = comp_v.shape[0]
    shard = comp_v.shape[2]
    cycles = leg_v.shape[1]
    slots = inv_v.shape[0]
    chunks = inv_v.shape[1] // 2
    rows = 4 * chans
    lanes = 4 * cycles
    total = chans * blks
    me_c = lax.axis_index("chan")
    me_b = lax.axis_index("blk")
    first = pl.multiple_of(me_c * shard, shard)

    me = me_b * chans + me_c

    def peer(offset):
        index = offset - 1 + (me < offset).astype(jnp.int32)
        return rest(index, chans), share(index, chans)

    def each(first_offset, last_offset, act):
        if last_offset - first_offset <= 64:
            for offset in range(first_offset, last_offset):
                act(offset)
        else:
            lax.fori_loop(
                first_offset, last_offset, lambda offset, carry: (act(offset), carry)[1], 0
            )

    barrier = pltpu.get_barrier_semaphore()

    def tell(semaphore, dest_c, dest_b):
        pl.semaphore_signal(
            semaphore,
            inc=1,
            device_id=(dest_c, dest_b),
            device_id_type=pl.DeviceIdType.MESH,
        )

    scalars = []

    def load(src, dst, group):
        copy = pltpu.make_async_copy(src, dst, in_sem.at[group])
        copy.start()
        return copy

    def loaded(dst, group):
        pltpu.make_async_copy(dst, dst, in_sem.at[group]).wait()

    for src, dst in (
        (order_hbm, order_s), (cycle_hbm, cycle_s), (pixel_hbm, pixel_s), (mix_hbm, mix_s),
        (chan_hbm, chan_s), (cycle_row_hbm, cycle_row),
    ):
        scalars.append(load(src, dst, 4 + len(scalars)))
    for kind in range(2):
        load(leg_hbm.at[kind, 0, :, pl.ds(first, shard)], leg_v.at[kind], 2)
    for comp in range(comps):
        for half in range(2):
            load(alm_hbm.at[comp, :, 0, :], comp_v.at[comp, pl.ds(4 * half, 4), :], 0)
    load(beam_hbm.at[:, pl.ds(first, shard)], beam_v, 1)
    for stokes in range(2):
        for slot in range(slots):
            load(
                inv_hbm.at[stokes, :, slot, :],
                inv_v.at[slot, pl.ds(stokes * chunks, chunks), :],
                3,
            )
    each(
        1,
        total,
        lambda offset: tell(
            barrier, rest(me_c + offset // blks, chans), rest(me_b + offset % blks, blks)
        ),
    )
    for copy in scalars:
        copy.wait()

    own_cycles = [cycle_s[me_b * slots + slot] for slot in range(slots)]
    own_pixels = [pixel_s[cycle].astype(F32) for cycle in own_cycles]

    def by_slot(slot_index, values):
        result = jnp.where(slot_index == 0, values[0], values[slots - 1])
        for slot in range(1, slots - 1):
            result = jnp.where(slot_index == slot, values[slot], result)
        return result

    grid = (blks, LANES)
    row = iota(grid, 0)
    lane = iota(grid, 1)
    orders = jnp.full(grid, order_s[0], jnp.int32)
    for order in range(1, blks):
        orders = jnp.where(row == order, order_s[order], orders)
    orders = orders.astype(F32)
    fine = orders * (2 * lane + 1).astype(F32)
    leap = orders * (2.0 * LANES)
    chunk = rest(lane, chunks).astype(F32)
    def table(slot):
        pixels = jnp.full(grid, own_pixels[slot], F32)
        reciprocal = 1.0 / pixels
        stride = leap - jnp.floor(leap * (0.5 * reciprocal)) * (2.0 * pixels)
        fine_turn = turn(fine, pixels, 2.0 * reciprocal)
        short = pixels <= float(LANES)
        fine_turn = [
            jnp.where(short, value.astype(BF16).astype(F32), value) for value in fine_turn
        ]
        coarse_turn = turn(stride * chunk, pixels, 2.0 * reciprocal)
        for order in range(blks):
            block = pl.ds(order * 4 * blks, 4 * blks)
            fine_v[slot, block, :] = jnp.concatenate(
                pair_turns(*fine_turn, order), axis=0
            ).astype(BF16)
            coarse_v[slot, block, :] = jnp.concatenate(pair_turns(*coarse_turn, order), axis=0)

    for slot in range(slots):
        table(slot)
    loaded(comp_v, 0)
    loaded(beam_v, 1)
    loaded(leg_v, 2)
    low_half = iota((8, 1), 0) < 4
    keep = (iota((1, shard), 1) + first >= order_s[me_b]).astype(F32)
    alm_rows = []
    for pair in range(chans // 2):
        picked = [chan_s[2 * pair], chan_s[2 * pair + 1]]
        columns = [
            jnp.where(low_half, mix_s[picked[0], comp], mix_s[picked[1], comp])
            for comp in range(comps)
        ]
        mixed = columns[0] * comp_v[0]
        for comp in range(1, comps):
            mixed = mixed + columns[comp] * comp_v[comp]
        gains = [beam_v[pl.ds(chan, 1), :] * keep for chan in picked]
        gain_v[pl.ds(2 * pair, 1), :] = gains[0]
        gain_v[pl.ds(2 * pair + 1, 1), :] = gains[1]
        alm_rows.append(mixed * jnp.where(low_half, gains[0], gains[1]))
    alm = jnp.concatenate(alm_rows, axis=0).astype(BF16)
    plus = dot(alm, jnp.concatenate([leg_v[0]] * 4, axis=0), NT)
    minus = dot(alm, jnp.concatenate([leg_v[1]] * 4, axis=0), NT)
    row_part = iota(plus.shape, 0) % 4
    lane_part = iota(plus.shape, 1) // cycles
    outer = (lane_part == 0) | (lane_part == 3)
    signed = jnp.where(outer, -minus, minus)
    joined = jnp.where(lane_part == row_part, plus, 0.0) + jnp.where(
        lane_part == 3 - row_part, signed, 0.0
    )
    folded = joined
    for step in range(1, 4):
        folded = folded + pltpu.roll(joined, rows - step, 0)
    for chan in range(chans):
        send1[pl.ds(chan, 1), :] = folded[4 * chan : 4 * chan + 1]


    def arrived(dst, phase):
        pltpu.make_async_copy(dst, dst, recv_sem.at[phase]).wait()

    def sent(dst, phase):
        pltpu.make_async_copy(dst, dst, send_sem.at[phase]).wait()

    def routes(dest_b):
        return (
            (send1, recv1.at[me_c, me_b]),
            (send2.at[dest_b], recv2.at[me_b, pl.ds(2 * me_c, 2), :]),
        )

    def post(offset, phase):
        dest_c, dest_b = peer(offset)
        src, dst = routes(dest_b)[phase]
        pltpu.make_async_remote_copy(
            src_ref=src,
            dst_ref=dst,
            send_sem=send_sem.at[phase],
            recv_sem=recv_sem.at[phase],
            device_id=(dest_c, dest_b),
            device_id_type=pl.DeviceIdType.MESH,
        ).start()

    early = min(3, total - 1)
    pl.semaphore_wait(barrier, total - 1)
    each(1, early + 1, lambda offset: post(offset, 0))
    loaded(inv_v, 3)
    grid = (2 * chunks, LANES)
    pixel_index = rest(iota(grid, 0), chunks) * LANES + iota(grid, 1)
    parts = [[] for _ in range(blks)]
    for slot in range(slots):
        live = pixel_index.astype(F32) < own_pixels[slot]
        noise = jnp.where(live, inv_v[slot], 0.0).astype(BF16)
        inner = dot(fine_v[slot], noise, NT)
        for order in range(blks):
            base = order * 4 * blks
            held = [inner[base + kind * blks : base + (kind + 1) * blks] for kind in range(4)]
            outer_turn = [
                coarse_v[slot, pl.ds(base + kind * blks, blks), :] for kind in range(4)
            ]
            add_real = outer_turn[0] * held[0] - outer_turn[1] * held[1]
            add_imag = outer_turn[0] * held[1] + outer_turn[1] * held[0]
            sub_real = outer_turn[2] * held[2] - outer_turn[3] * held[3]
            sub_imag = outer_turn[2] * held[3] + outer_turn[3] * held[2]
            blocks = jnp.concatenate(
                [
                    sub_real + add_real,
                    sub_imag - add_imag,
                    -sub_imag - add_imag,
                    sub_real - add_real,
                ],
                axis=0,
            )
            high = blocks.astype(BF16)
            parts[order].append((high, (blocks - high.astype(F32)).astype(BF16)))
    ones = (
        share(rest(iota((8, 2 * LANES), 1), LANES), chunks) == iota((8, 2 * LANES), 0)
    ).astype(F32).astype(BF16)
    weight = 0.5 / by_slot(share(iota((2, lanes), 1), 4 * blks), own_pixels)
    for order in range(blks):
        halves = [jnp.concatenate(pair, axis=1) for pair in parts[order]]
        summed = dot(ones, jnp.concatenate(halves, axis=0), NT)
        send2[order] = summed[0:2] * weight
    each(1, early + 1, lambda offset: post(offset, 1))
    each(early + 1, total, lambda offset: (post(offset, 0), post(offset, 1)))
    for phase, (src, dst) in enumerate(routes(me_b)):
        pltpu.make_async_copy(src, dst, recv_sem.at[phase]).start()
        pltpu.make_async_copy(src, (spare1, spare2)[phase], send_sem.at[phase]).start()

    to_lane = iota((cycles, lanes), 1)
    spread = (
        iota((cycles, lanes), 0) == rest(to_lane, blks) * slots + share(to_lane, 4 * blks)
    ).astype(F32).astype(BF16)
    lane_cycle = dot(
        jnp.broadcast_to(cycle_row[...].astype(F32), (8, cycles)).astype(BF16), spread, NN
    )[0:1]
    half = (2 * cycles, lanes)
    from_row = iota(half, 0)
    shuffle = (
        (rest(from_row, cycles).astype(F32) == lane_cycle)
        & (share(from_row, cycles) == (share(iota(half, 1), blks) & 1))
    ).astype(F32)
    leg_stack = jnp.concatenate([leg_v[0], leg_v[1]], axis=0)
    back_leg = dot(shuffle.T.astype(BF16), leg_stack, NN).astype(BF16)
    empty = jnp.zeros(half, F32)
    shuffle = jnp.concatenate(
        [
            jnp.concatenate([shuffle, empty], axis=1),
            jnp.concatenate([empty, shuffle], axis=1),
        ],
        axis=0,
    ).astype(BF16)

    arrived(recv1, 0)
    gathered = []
    for order in range(blks):
        coeffs = recv1[0, order]
        for chan in range(1, chans):
            coeffs = coeffs + recv1[chan, order]
        gathered.append(coeffs)
    coeffs = dot(jnp.concatenate(gathered, axis=0).astype(BF16), shuffle, NN)
    for order in range(blks):
        own = coeffs[order * chans : (order + 1) * chans]
        for tile in range(lanes // LANES):
            for part in range(2):
                begin = part * lanes + tile * LANES
                twin_v[order, tile, pl.ds(part, chans, stride=2), :] = own[
                    :, begin : begin + LANES
                ]
    turned = [
        jnp.concatenate([twin_v[order, tile] for tile in range(lanes // LANES)], axis=1)
        for order in range(blks)
    ]
    low_lane = iota((2 * chans, lanes), 1)
    step = 1
    while step < blks:
        upper = (share(low_lane, step) & 1) == 1
        following = list(turned)
        for order in range(blks):
            if (order // step) % 2 == 0:
                one, two = turned[order], turned[order + step]
                following[order] = jnp.where(upper, pltpu.roll(two, step, 1), one)
                following[order + step] = jnp.where(
                    upper, two, pltpu.roll(one, lanes - step, 1)
                )
        turned = following
        step *= 2

    final_row = iota((8, lanes), 0)
    final_lane = iota((8, lanes), 1)
    row_real = final_row & 1
    row_stokes = (final_row >> 1) & 1
    lane_kind = share(final_lane, blks) & 1
    lane_real = share(final_lane, 2 * blks) & 1
    straight = (lane_kind == 0) & (lane_real == row_real)
    crossed = (lane_kind == 1) & (lane_real != row_real)
    cross_sign = jnp.where(row_stokes == row_real, -1.0, 1.0)
    mask = [
        jnp.where(straight & (row_stokes == stokes), 1.0, 0.0)
        + jnp.where(crossed & (row_stokes != stokes), cross_sign, 0.0)
        for stokes in range(2)
    ]

    arrived(recv2, 1)
    sums = [recv2[block] * turned[block] for block in range(blks)]
    step = blks // 2
    while step >= 1:
        upper = (share(low_lane, step) & 1) == 1
        merged = []
        for block in range(step):
            one, two = sums[block], sums[block + step]
            kept = jnp.where(upper, two, one)
            moved = jnp.where(upper, one, two)
            merged.append(
                kept
                + jnp.where(
                    upper, pltpu.roll(moved, step, 1), pltpu.roll(moved, lanes - step, 1)
                )
            )
        sums = merged
        step //= 2
    total_sum = sums[0]
    odd_part = (share(iota(total_sum.shape, 1), blks) & 1) == 1
    total_sum = total_sum + jnp.where(
        odd_part, pltpu.roll(total_sum, blks, 1), pltpu.roll(total_sum, lanes - blks, 1)
    )
    total_sum = total_sum.astype(BF16).astype(F32)
    left = jnp.concatenate(
        [
            mask[0] * total_sum[2 * chan : 2 * chan + 1]
            + mask[1] * total_sum[2 * chan + 1 : 2 * chan + 2]
            for chan in range(chans)
        ],
        axis=0,
    )
    alm_grads = dot(left.astype(BF16), back_leg, NN)
    scaled = [
        alm_grads[8 * chan : 8 * chan + 8] * gain_v[pl.ds(chan, 1), :] for chan in range(chans)
    ]
    for comp in range(comps):
        mixed = mix_s[chan_s[0], comp] * scaled[0]
        for chan in range(1, chans):
            mixed = mixed + mix_s[chan_s[chan], comp] * scaled[chan]
        out_ref[comp] = mixed[0:4]
    sent(recv1, 0)
    sent(recv2, 1)


def body(
    chans, blks, comp_alms, legendre, inv_noise, beam_window, mixing, channel_of, m_orders,
    cycle_of, cycle_pixels,
):
    comps, parts, order_dev, shard = comp_alms.shape
    cycles = legendre.shape[3]
    chan_dev, stokes, slots, width = inv_noise.shape
    assert parts == 4 and stokes == 2 and order_dev == 1 and chan_dev == 1
    lanes = 4 * cycles
    assert slots * blks == cycles
    chunks = width // LANES
    assert 2 * chunks == LANES
    noise = jnp.swapaxes(inv_noise.reshape(stokes, slots, chunks, LANES), 1, 2)
    any_space = pl.BlockSpec(memory_space=pl.ANY)
    vector = pl.BlockSpec(memory_space=pltpu.VMEM)
    result = pl.pallas_call(
        functools.partial(kernel, chans, blks),
        out_shape=pltpu.VMEM((comps, 4, shard), F32),
        in_specs=[any_space] * 10,
        out_specs=vector,
        scratch_shapes=[
            pltpu.SMEM(mixing.shape, F32),
            pltpu.SMEM(channel_of.shape, jnp.int32),
            pltpu.SMEM(m_orders.shape, jnp.int32),
            pltpu.SMEM(cycle_of.shape, jnp.int32),
            pltpu.SMEM(cycle_pixels.shape, jnp.int32),
            pltpu.VMEM((1, cycles), jnp.int32),
            pltpu.VMEM((comps, 8, shard), F32),
            pltpu.VMEM((2, cycles, shard), BF16),
            pltpu.VMEM((slots, 2 * chunks, LANES), F32),
            pltpu.VMEM((beam_window.shape[0], shard), F32),
            pltpu.VMEM((chans, shard), F32),
            pltpu.VMEM((slots, 4 * blks * blks, LANES), BF16),
            pltpu.VMEM((slots, 4 * blks * blks, LANES), F32),
            pltpu.VMEM((chans, lanes), F32),
            pltpu.VMEM((chans, blks, chans, lanes), F32),
            pltpu.VMEM((blks, 2, lanes), F32),
            pltpu.VMEM((blks, 2 * chans, lanes), F32),
            pltpu.VMEM((chans, lanes), F32),
            pltpu.VMEM((2, lanes), F32),
            pltpu.VMEM((blks, lanes // LANES, 2 * chans, LANES), F32),
            pltpu.SemaphoreType.DMA((10,)),
            pltpu.SemaphoreType.DMA((2,)),
            pltpu.SemaphoreType.DMA((2,)),
        ],
        compiler_params=pltpu.CompilerParams(collective_id=0, has_side_effects=True),
        name="normal_product",
    )(
        comp_alms, jnp.swapaxes(legendre, 2, 3), noise, beam_window, mixing, channel_of,
        m_orders, cycle_of, cycle_pixels, cycle_of.reshape(1, cycles),
    )
    return result.reshape(comp_alms.shape)


def solution(mesh):
    in_specs = (
        P(None, None, "blk", "chan"),
        P(None, "blk", None, None),
        P("chan", None, "blk", None),
        P(),
        P(),
        P(),
        P(),
        P(),
        P(),
    )
    out_specs = P(None, None, "blk", "chan")
    work = functools.partial(body, mesh.shape["chan"], mesh.shape["blk"])
    return jax.shard_map(work, mesh=mesh, in_specs=in_specs, out_specs=out_specs, check_vma=False)
```
